512 devices in a mesh: view: 8 (over y, core), scene: 64 (over x, z).
Axes of the slice: x: 4, y: 4, z: 16, core: 2. Of those that a mesh axis runs over, the one named last changes fastest.
Arguments:
- means: float32 [1024, 3, 128], P(('view', 'scene')), may hold values from -3 to 3
- log_scales: float32 [1024, 3, 128], P(('view', 'scene')), may hold values from -3.3 to -0.4, as said below
- rotations: float32 [1024, 4, 128], P(('view', 'scene')), may hold values from -2.5 to 2.5
- opacity_logits: float32 [1024, 1, 128], P(('view', 'scene')), may hold values from -3 to 3
- colour_coefs: float32 [1024, 48, 128], P(('view', 'scene')), may hold values from -2 to 2
- cameras: float32 [8, 16], replicated, may hold values from -1 to 2048, as said below
- exposure: float32 [8, 12], P('view'), may hold values from -1 to 1
- target: float32 [8, 1024, 3, 256], P('view', 'scene'), may hold values from 0 to 1
- tile_ids: int32 [8, 1024], P('view', 'scene'), may hold values from 0 to 1023, each once within a row
- send_list: int32 [8, 64, 64, 2], P('view', 'scene'), may hold values from -1 to 15, as said below
- pair_slots: int32 [8, 1024, 4], P('view', 'scene'), may hold values from -1 to 127, as said below
Outputs:
- shown: float32 [8, 1024, 3, 256], P('view', 'scene')
- grad_means: float32 [1024, 3, 128], P(('view', 'scene'))
- grad_log_scales: float32 [1024, 3, 128], P(('view', 'scene'))
- grad_rotations: float32 [1024, 4, 128], P(('view', 'scene'))
- grad_opacity: float32 [1024, 1, 128], P(('view', 'scene'))
- grad_colour: float32 [1024, 48, 128], P(('view', 'scene'))
- grad_exposure: float32 [8, 12], P('view')
The draws below stay inside these ranges and needn't reach their ends.
Inputs may be any that keep to these rules, and one draw needn't show every extreme that they name: send_list[v, s, r, c] is a local block number of owner s or -1; in each row of 2 the live entries come first and are all different, and a row may have none; in every image some renderer gets 2 blocks from every owner. pair_slots[v, t, k] is -1 or s * 2 + c with c below the number of live entries of send_list[v, s, t // 16]; a tile's live entries come first, at least one, all different; in every image each renderer has a tile with 4 live entries. `cameras`: each row is a rotation matrix, a translation, two focal lengths and a principal point; every Gaussian lies at depth 4 or more before each camera. `log_scales`: logarithms of lengths in world units.
All inputs are finite; a program needn't handle non-finite values.
Results may differ from the reference program's by a relative error of at most 0.0003.
Values sent between devices are 32-bit elements; how exact they have to be, the bound alone decides.
No kernel may reach another device: no remote copies, remote signals or barrier semaphores. Data moves between devices by JAX's collectives and lax.ppermute only.
A program may use at most 64 MiB of HBM per device.

```python
import jax
import jax.numpy as jnp
from jax import lax

G = 128
PIX = 256
KMAX = 4
CAP = 2
TILE_COLS = 32
BLK_DEV = 2
TILES_DEV = 16
BLOCKS = 1024
TILES = 1024
N_VIEW = 8
N_SCENE = 64


def routing(key):
    keys = [jax.random.fold_in(key, 11 + step_at) for step_at in range(6)]
    pick_total = TILES_DEV * KMAX
    owner_scores = jax.random.randint(keys[0], (N_VIEW, N_SCENE, TILES_DEV, N_SCENE), 0, 1 << 20) * N_SCENE + jnp.arange(N_SCENE, dtype=jnp.int32)
    owners = lax.top_k(owner_scores, KMAX)[1].astype(jnp.int32)
    tile_count = jax.random.randint(keys[1], (N_VIEW, N_SCENE, TILES_DEV), 1, KMAX + 1)
    full_tile = jax.random.randint(keys[2], (N_VIEW, N_SCENE), 0, TILES_DEV)
    tile_count = jnp.where(jnp.arange(TILES_DEV)[None, None, :] == full_tile[:, :, None], KMAX, tile_count)
    live_pick = (jnp.arange(KMAX)[None, None, None, :] < tile_count[..., None]).reshape(N_VIEW, N_SCENE, pick_total)
    flat_owner = owners.reshape(N_VIEW, N_SCENE, pick_total)
    same_owner = (flat_owner[..., :, None] == flat_owner[..., None, :]) & live_pick[..., :, None]
    pick_index = jnp.arange(pick_total)
    earlier = pick_index[:, None] < pick_index[None, :]
    occurrence = jnp.sum((same_owner & earlier[None, None]).astype(jnp.int32), axis=-2)
    place = occurrence % CAP
    owner_hits = jnp.sum(((flat_owner[..., None] == jnp.arange(N_SCENE)[None, None, None, :]) & live_pick[..., None]).astype(jnp.int32), axis=-2)
    counts = jnp.minimum(owner_hits, CAP)
    hot = jax.random.randint(keys[3], (N_VIEW,), 0, N_SCENE)
    counts = jnp.where(jnp.arange(N_SCENE)[None, :, None] == hot[:, None, None], CAP, counts)
    counts = jnp.transpose(counts, (0, 2, 1))
    owned_count = BLK_DEV * N_VIEW
    scores = jax.random.randint(keys[4], (N_VIEW, N_SCENE, N_SCENE, owned_count), 0, 1 << 20) * owned_count + jnp.arange(owned_count)
    order = jnp.argsort(scores, axis=-1)[..., :CAP].astype(jnp.int32)
    live_send = jnp.arange(CAP)[None, None, None, :] < counts[..., None]
    send = jnp.where(live_send, order, -1).astype(jnp.int32)
    pairs = jnp.where(live_pick, flat_owner * CAP + place, -1)
    return (send, pairs.reshape(N_VIEW, N_SCENE * TILES_DEV, KMAX).astype(jnp.int32))


def draw_send_list(key, part):
    return routing(jax.random.fold_in(key, 5))[0]


def draw_pair_slots(key, part):
    return routing(jax.random.fold_in(key, 5))[1]


def draw_log_scales(key, part):
    long_axis = jax.random.uniform(jax.random.fold_in(key, 61), (BLOCKS, 1, G), jnp.float32, -1.0, -0.4)
    short_axes = jax.random.uniform(jax.random.fold_in(key, 62), (BLOCKS, 2, G), jnp.float32, -3.3, -2.7)
    return jnp.concatenate([long_axis, short_axes], axis=1)


def draw_cameras(key, part):
    keys = [jax.random.fold_in(key, 41 + step_at) for step_at in range(5)]
    quat = jax.random.uniform(keys[0], (N_VIEW, 4), jnp.float32, -1.0, 1.0)
    quat = quat + jnp.array([2.0, 0.0, 0.0, 0.0], jnp.float32)
    quat = quat / jnp.sqrt(jnp.sum(quat * quat, axis=1, keepdims=True))
    quat_w, quat_x, quat_y, quat_z = (quat[:, 0], quat[:, 1], quat[:, 2], quat[:, 3])
    rotation = jnp.stack([1.0 - 2.0 * (quat_y * quat_y + quat_z * quat_z), 2.0 * (quat_x * quat_y - quat_w * quat_z), 2.0 * (quat_x * quat_z + quat_w * quat_y), 2.0 * (quat_x * quat_y + quat_w * quat_z), 1.0 - 2.0 * (quat_x * quat_x + quat_z * quat_z), 2.0 * (quat_y * quat_z - quat_w * quat_x), 2.0 * (quat_x * quat_z - quat_w * quat_y), 2.0 * (quat_y * quat_z + quat_w * quat_x), 1.0 - 2.0 * (quat_x * quat_x + quat_y * quat_y)], axis=1)
    shift_side = jax.random.uniform(keys[1], (N_VIEW, 2), jnp.float32, -0.5, 0.5)
    shift_depth = jax.random.uniform(keys[2], (N_VIEW, 1), jnp.float32, 10.0, 12.0)
    image_width = TILE_COLS * 16.0
    image_height = TILES // TILE_COLS * 16.0
    focal = jax.random.uniform(keys[3], (N_VIEW, 1), jnp.float32, 0.9, 1.1) * image_width * 10.0 / 6.0
    centre = jax.random.uniform(keys[4], (N_VIEW, 2), jnp.float32, 0.95, 1.05) * jnp.array([image_width / 2.0, image_height / 2.0], jnp.float32)
    return jnp.concatenate([rotation, shift_side, shift_depth, focal, focal, centre], axis=1)


def shard_levels(key, extent, cuts, least, top_value):
    factor_of, own = 1.0, jax.random.fold_in(key, 6)
    for dim, blocks in cuts:
        steps = jnp.exp(jax.random.uniform(jax.random.fold_in(own, dim), (blocks,), jnp.float32, least / len(cuts), top_value / len(cuts)))
        factor_of = factor_of * jnp.repeat(steps, extent[dim] // blocks).reshape([-1 if axis == dim else 1 for axis in range(len(extent))])
    return factor_of


def scatter_about(stream_key, extent, width, most, shards=(), kind=jnp.bfloat16):
    result = jax.random.normal(stream_key, extent, jnp.float32) * width
    if len(shards) > 0:
        result = shard_levels(stream_key, extent, shards, -0.22, 0.18) * result
    return jnp.clip(result, min=-most, max=most).astype(kind)


def setup_inputs(seed: int = 0) -> dict:
    arg_keys = jax.random.split(jax.random.key(seed), 12)
    means = jnp.clip(jax.random.uniform(arg_keys[0], (BLOCKS, 3, G), jnp.float32, -3.0, 3.0) * shard_levels(arg_keys[0], (BLOCKS, 3, G), ((0, 512),), -0.4, 0.0), -3.0, 3.0)
    log_scales = draw_log_scales(jax.random.fold_in(arg_keys[11], 71), 0)
    rotations = scatter_about(arg_keys[2], (BLOCKS, 4, G), 1.0, 2.5, ((0, 512),), jnp.float32)
    opacity_logits = jnp.clip(jax.random.uniform(arg_keys[3], (BLOCKS, 1, G), jnp.float32, -3.0, 3.0) * shard_levels(arg_keys[3], (BLOCKS, 1, G), ((0, 512),), -0.4, 0.0), -3.0, 3.0)
    colour_coefs = scatter_about(arg_keys[4], (BLOCKS, 48, G), 0.25, 2.0, ((0, 512),), jnp.float32)
    cameras = draw_cameras(jax.random.fold_in(arg_keys[11], 71), 0)
    exposure = scatter_about(arg_keys[6], (N_VIEW, 12), 0.3, 1.0, ((0, 8),), jnp.float32)
    target = jnp.clip(1.0 * jax.random.uniform(arg_keys[7], (N_VIEW, TILES, 3, PIX), jnp.float32) ** shard_levels(arg_keys[7], (N_VIEW, TILES, 3, PIX), ((0, 8), (1, 64)), -0.2, 0.2), 0.0, 1.0)
    tile_ids = jax.vmap(lambda own: jax.random.permutation(own, TILES))(jax.random.split(arg_keys[8], N_VIEW)).reshape((N_VIEW, TILES)).astype(jnp.int32)
    send_list = draw_send_list(jax.random.fold_in(arg_keys[11], 71), 0)
    pair_slots = draw_pair_slots(jax.random.fold_in(arg_keys[11], 71), 0)
    return {"means": means, "log_scales": log_scales, "rotations": rotations, "opacity_logits": opacity_logits, "colour_coefs": colour_coefs, "cameras": cameras, "exposure": exposure, "target": target, "tile_ids": tile_ids, "send_list": send_list, "pair_slots": pair_slots}


SH_ZERO = 0.28209479177387814
SH_ONE = 0.4886025119029199
SH_TWO = (1.0925484305920792, -1.0925484305920792, 0.31539156525252005, -1.0925484305920792, 0.5462742152960396)
SH_THREE = (-0.5900435899266435, 2.890611442640554, -0.4570457994644658, 0.3731763325901154, -0.4570457994644658, 1.445305721320277, -0.5900435899266435)

def harmonics(dir_x, dir_y, dir_z):
    sq_x, sq_y, sq_z = (dir_x * dir_x, dir_y * dir_y, dir_z * dir_z)
    sh_basis = [SH_ZERO * jnp.ones_like(dir_x), -SH_ONE * dir_y, SH_ONE * dir_z, -SH_ONE * dir_x, SH_TWO[0] * dir_x * dir_y, SH_TWO[1] * dir_y * dir_z, SH_TWO[2] * (2.0 * sq_z - sq_x - sq_y), SH_TWO[3] * dir_x * dir_z, SH_TWO[4] * (sq_x - sq_y), SH_THREE[0] * dir_y * (3.0 * sq_x - sq_y), SH_THREE[1] * dir_x * dir_y * dir_z, SH_THREE[2] * dir_y * (4.0 * sq_z - sq_x - sq_y), SH_THREE[3] * dir_z * (2.0 * sq_z - 3.0 * sq_x - 3.0 * sq_y), SH_THREE[4] * dir_x * (4.0 * sq_z - sq_x - sq_y), SH_THREE[5] * dir_z * (sq_x - sq_y), SH_THREE[6] * dir_x * (sq_x - 3.0 * sq_y)]
    return jnp.stack(sh_basis, axis=1)

def project(pieces, camera):
    means, log_scales, rotations, opacity_logits, colour_coefs = pieces
    rotation = camera[0:9].reshape(3, 3)
    translation = camera[9:12]
    focal_x, focal_y, centre_x, centre_y = (camera[12], camera[13], camera[14], camera[15])
    position = [means[:, 0], means[:, 1], means[:, 2]]
    view_pos = [rotation[row_at, 0] * position[0] + rotation[row_at, 1] * position[1] + rotation[row_at, 2] * position[2] + translation[row_at] for row_at in range(3)]
    inv_depth = 1.0 / view_pos[2]
    quat_w = rotations[:, 0] + 3.0
    quat_x, quat_y, quat_z = (rotations[:, 1], rotations[:, 2], rotations[:, 3])
    quat_norm = jnp.sqrt(quat_w * quat_w + quat_x * quat_x + quat_y * quat_y + quat_z * quat_z)
    quat_w, quat_x, quat_y, quat_z = (quat_w / quat_norm, quat_x / quat_norm, quat_y / quat_norm, quat_z / quat_norm)
    spin_matrix = [[1.0 - 2.0 * (quat_y * quat_y + quat_z * quat_z), 2.0 * (quat_x * quat_y - quat_w * quat_z), 2.0 * (quat_x * quat_z + quat_w * quat_y)], [2.0 * (quat_x * quat_y + quat_w * quat_z), 1.0 - 2.0 * (quat_x * quat_x + quat_z * quat_z), 2.0 * (quat_y * quat_z - quat_w * quat_x)], [2.0 * (quat_x * quat_z - quat_w * quat_y), 2.0 * (quat_y * quat_z + quat_w * quat_x), 1.0 - 2.0 * (quat_x * quat_x + quat_y * quat_y)]]
    scales = jnp.exp(log_scales)
    world_frame = [[spin_matrix[row_at][col_at] * scales[:, col_at] for col_at in range(3)] for row_at in range(3)]
    jacobian = [[focal_x * inv_depth * rotation[0, col_at] - focal_x * view_pos[0] * inv_depth * inv_depth * rotation[2, col_at] for col_at in range(3)], [focal_y * inv_depth * rotation[1, col_at] - focal_y * view_pos[1] * inv_depth * inv_depth * rotation[2, col_at] for col_at in range(3)]]
    screen_frame = [[jacobian[row_at][0] * world_frame[0][col_at] + jacobian[row_at][1] * world_frame[1][col_at] + jacobian[row_at][2] * world_frame[2][col_at] for col_at in range(3)] for row_at in range(2)]
    sigma_xx = screen_frame[0][0] ** 2 + screen_frame[0][1] ** 2 + screen_frame[0][2] ** 2 + 0.3
    sigma_yy = screen_frame[1][0] ** 2 + screen_frame[1][1] ** 2 + screen_frame[1][2] ** 2 + 0.3
    sigma_xy = screen_frame[0][0] * screen_frame[1][0] + screen_frame[0][1] * screen_frame[1][1] + screen_frame[0][2] * screen_frame[1][2]
    determinant = sigma_xx * sigma_yy - sigma_xy * sigma_xy
    screen_x = focal_x * view_pos[0] * inv_depth + centre_x
    screen_y = focal_y * view_pos[1] * inv_depth + centre_y
    opacity = jax.nn.sigmoid(opacity_logits[:, 0])
    eye_pos = [-(rotation[0, col_at] * translation[0] + rotation[1, col_at] * translation[1] + rotation[2, col_at] * translation[2]) for col_at in range(3)]
    offsets = [position[col_at] - eye_pos[col_at] for col_at in range(3)]
    eye_dist = jnp.sqrt(offsets[0] ** 2 + offsets[1] ** 2 + offsets[2] ** 2)
    sh_basis = harmonics(offsets[0] / eye_dist, offsets[1] / eye_dist, offsets[2] / eye_dist)
    sh_coefs = colour_coefs.reshape(colour_coefs.shape[0], 16, 3, colour_coefs.shape[2])
    colour = jnp.maximum(0.5 + lax.optimization_barrier(jnp.sum(sh_basis[:, :, None, :] * sh_coefs, axis=1)), 0.0)
    shape_rows = jnp.stack([screen_x, screen_y, sigma_yy / determinant, -sigma_xy / determinant, sigma_xx / determinant, opacity], axis=1)
    return jnp.concatenate([shape_rows, colour], axis=1)

def composite(chosen_blk, live_mask, tile_id):
    pixel_index = jnp.arange(PIX, dtype=jnp.int32)
    pixel_x = (16 * (tile_id % TILE_COLS) + pixel_index % 16).astype(jnp.float32) + 0.5
    pixel_y = (16 * (tile_id // TILE_COLS) + pixel_index // 16).astype(jnp.float32) + 0.5
    gap_x = pixel_x[None, :, None] - chosen_blk[:, 0][:, None, :]
    gap_y = pixel_y[None, :, None] - chosen_blk[:, 1][:, None, :]
    falloff = 0.5 * (chosen_blk[:, 2][:, None, :] * gap_x * gap_x + chosen_blk[:, 4][:, None, :] * gap_y * gap_y) + chosen_blk[:, 3][:, None, :] * gap_x * gap_y
    alpha_vals = chosen_blk[:, 5][:, None, :] * jnp.exp(-falloff) * live_mask.astype(jnp.float32)[:, None, None]
    log_keep = jnp.log1p(-alpha_vals)
    slot_count, pixel_count, lane_count = log_keep.shape
    flat_keep = jnp.transpose(log_keep, (1, 0, 2)).reshape(pixel_count, slot_count * lane_count)
    before_sum = jnp.cumsum(flat_keep, axis=1) - flat_keep
    transmit = jnp.transpose(jnp.exp(before_sum).reshape(pixel_count, slot_count, lane_count), (1, 0, 2))
    return jnp.einsum('kpg,kcg->cp', alpha_vals * transmit, chosen_blk[:, 6:9], precision=lax.Precision.HIGHEST)

def reference(means, log_scales, rotations, opacity_logits, colour_coefs, cameras, exposure, target, tile_ids, send_list, pair_slots):
    renderer = jnp.arange(TILES, dtype=jnp.int32) // TILES_DEV
    safe_slot = jnp.maximum(pair_slots, 0)
    source = safe_slot // CAP
    place = safe_slot % CAP
    view_rows = jnp.arange(N_VIEW, dtype=jnp.int32)[:, None, None]
    local_ids = send_list[view_rows, source, renderer[None, :, None], place]
    block_ids = (local_ids // BLK_DEV * (N_SCENE * BLK_DEV) + source * BLK_DEV + local_ids % BLK_DEV).astype(jnp.int32)
    live_mask = pair_slots >= 0

    def forward(pieces, expo_all):

        def one_view(view_items):
            camera, expo, view_blocks, view_live, view_tiles = view_items
            projected = project(pieces, camera)

            def one_tile(tile_items):
                return composite(jnp.take(projected, tile_items[0], axis=0), tile_items[1], tile_items[2])
            shaded = lax.map(jax.checkpoint(one_tile), (view_blocks, view_live, view_tiles))
            mixing = jnp.eye(3, dtype=jnp.float32) + expo[0:9].reshape(3, 3)
            return jnp.einsum('ij,tjp->tip', mixing, shaded, precision=lax.Precision.HIGHEST) + expo[9:12][None, :, None]
        return lax.map(one_view, (cameras, expo_all, block_ids, live_mask, tile_ids))
    params = (means, log_scales, rotations, opacity_logits, colour_coefs)
    shown, backward = jax.vjp(forward, params, exposure)
    param_grads, grad_exposure = backward(shown - target)
    return (shown, param_grads[0], param_grads[1], param_grads[2], param_grads[3], param_grads[4], grad_exposure)
```

```python
import jax
import jax.numpy as jnp
from jax import lax
from jax.experimental import pallas as pl
from jax.experimental.pallas import tpu as pltpu
from jax.sharding import PartitionSpec as P

PIX = 256
TILE_COLS = 32
G = 128
FEAT = 9
F32 = jnp.float32
BF16 = jnp.bfloat16
LOG2E = 1.4426950408889634

SH_ZERO = 0.28209479177387814
SH_ONE = 0.4886025119029199
SH_TWO = (
    1.0925484305920792,
    -1.0925484305920792,
    0.31539156525252005,
    -1.0925484305920792,
    0.5462742152960396,
)
SH_THREE = (
    -0.5900435899266435,
    2.890611442640554,
    -0.4570457994644658,
    0.3731763325901154,
    -0.4570457994644658,
    1.445305721320277,
    -0.5900435899266435,
)


def harmonics(dir_x, dir_y, dir_z):
    sq_x, sq_y, sq_z = (dir_x * dir_x, dir_y * dir_y, dir_z * dir_z)
    return [
        SH_ZERO * jnp.ones_like(dir_x),
        -SH_ONE * dir_y,
        SH_ONE * dir_z,
        -SH_ONE * dir_x,
        SH_TWO[0] * dir_x * dir_y,
        SH_TWO[1] * dir_y * dir_z,
        SH_TWO[2] * (2.0 * sq_z - sq_x - sq_y),
        SH_TWO[3] * dir_x * dir_z,
        SH_TWO[4] * (sq_x - sq_y),
        SH_THREE[0] * dir_y * (3.0 * sq_x - sq_y),
        SH_THREE[1] * dir_x * dir_y * dir_z,
        SH_THREE[2] * dir_y * (4.0 * sq_z - sq_x - sq_y),
        SH_THREE[3] * dir_z * (2.0 * sq_z - 3.0 * sq_x - 3.0 * sq_y),
        SH_THREE[4] * dir_x * (4.0 * sq_z - sq_x - sq_y),
        SH_THREE[5] * dir_z * (sq_x - sq_y),
        SH_THREE[6] * dir_x * (sq_x - 3.0 * sq_y),
    ]


def project(position, log_scales, quats, logit, coefs, cam):
    rotation = [[cam[3 * row + col] for col in range(3)] for row in range(3)]
    translation = cam[9:12]
    focal_x, focal_y, centre_x, centre_y = cam[12:16]
    view_pos = [
        rotation[row][0] * position[0]
        + rotation[row][1] * position[1]
        + rotation[row][2] * position[2]
        + translation[row]
        for row in range(3)
    ]
    inv_depth = 1.0 / view_pos[2]
    quat_w = quats[0] + 3.0
    quat_x, quat_y, quat_z = quats[1:4]
    quat_norm = jnp.sqrt(quat_w * quat_w + quat_x * quat_x + quat_y * quat_y + quat_z * quat_z)
    inv_norm = 1.0 / quat_norm
    quat_w, quat_x, quat_y, quat_z = (
        quat_w * inv_norm,
        quat_x * inv_norm,
        quat_y * inv_norm,
        quat_z * inv_norm,
    )
    spin = [
        [
            1.0 - 2.0 * (quat_y * quat_y + quat_z * quat_z),
            2.0 * (quat_x * quat_y - quat_w * quat_z),
            2.0 * (quat_x * quat_z + quat_w * quat_y),
        ],
        [
            2.0 * (quat_x * quat_y + quat_w * quat_z),
            1.0 - 2.0 * (quat_x * quat_x + quat_z * quat_z),
            2.0 * (quat_y * quat_z - quat_w * quat_x),
        ],
        [
            2.0 * (quat_x * quat_z - quat_w * quat_y),
            2.0 * (quat_y * quat_z + quat_w * quat_x),
            1.0 - 2.0 * (quat_x * quat_x + quat_y * quat_y),
        ],
    ]
    scales = [jnp.exp(row) for row in log_scales]
    world = [[spin[row][col] * scales[col] for col in range(3)] for row in range(3)]
    step_x = focal_x * inv_depth
    step_y = focal_y * inv_depth
    slide_x = step_x * view_pos[0] * inv_depth
    slide_y = step_y * view_pos[1] * inv_depth
    jac = [
        [step_x * rotation[0][col] - slide_x * rotation[2][col] for col in range(3)],
        [step_y * rotation[1][col] - slide_y * rotation[2][col] for col in range(3)],
    ]
    screen = [
        [
            jac[row][0] * world[0][col] + jac[row][1] * world[1][col] + jac[row][2] * world[2][col]
            for col in range(3)
        ]
        for row in range(2)
    ]
    sigma_xx = screen[0][0] * screen[0][0] + screen[0][1] * screen[0][1] + screen[0][2] * screen[0][2] + 0.3
    sigma_yy = screen[1][0] * screen[1][0] + screen[1][1] * screen[1][1] + screen[1][2] * screen[1][2] + 0.3
    sigma_xy = screen[0][0] * screen[1][0] + screen[0][1] * screen[1][1] + screen[0][2] * screen[1][2]
    inv_det = 1.0 / (sigma_xx * sigma_yy - sigma_xy * sigma_xy)
    screen_x = step_x * view_pos[0] + centre_x
    screen_y = step_y * view_pos[1] + centre_y
    opacity = 1.0 / (1.0 + jnp.exp(-logit))
    eye = [
        -(
            rotation[0][col] * translation[0]
            + rotation[1][col] * translation[1]
            + rotation[2][col] * translation[2]
        )
        for col in range(3)
    ]
    offs = [position[col] - eye[col] for col in range(3)]
    inv_dist = 1.0 / jnp.sqrt(offs[0] * offs[0] + offs[1] * offs[1] + offs[2] * offs[2])
    basis = harmonics(offs[0] * inv_dist, offs[1] * inv_dist, offs[2] * inv_dist)
    colours = []
    for channel in range(3):
        total = basis[0] * coefs[channel]
        for band in range(1, 16):
            total = total + basis[band] * coefs[3 * band + channel]
        colours.append(jnp.maximum(0.5 + total, 0.0))
    return [
        screen_x,
        screen_y,
        sigma_yy * inv_det,
        -sigma_xy * inv_det,
        sigma_xx * inv_det,
        opacity,
    ] + colours


def block_inputs(refs, block, views):
    means, log_scales, rotations, logits, coefs = refs

    def rows(ref, count):
        return [jnp.broadcast_to(ref[block, pl.ds(r, 1), :], (views, G)) for r in range(count)]

    return (rows(means, 3), rows(log_scales, 3), rows(rotations, 4), rows(logits, 1)[0], rows(coefs, 48))


def camera_columns(cam_ref, views):
    cams = cam_ref[...]
    return [jnp.broadcast_to(cams[:, col : col + 1], (views, G)) for col in range(16)]


def project_kernel(means, log_scales, rotations, logits, coefs, cam_ref, out_ref):
    views = cam_ref.shape[0]
    blocks = means.shape[0]
    cam = camera_columns(cam_ref, views)
    for block in range(blocks):
        pieces = block_inputs((means, log_scales, rotations, logits, coefs), block, views)
        for feat, value in enumerate(project(*pieces, cam)):
            out_ref[pl.ds(block * FEAT + feat, views, stride=blocks * FEAT), :] = value


def unproject_kernel(
    means, log_scales, rotations, logits, coefs, cam_ref, back_ref, o_means, o_scales, o_rot, o_logit, o_coef
):
    views = cam_ref.shape[0]
    blocks = means.shape[0]
    cam = camera_columns(cam_ref, views)

    def total(value):
        return jnp.sum(value, axis=0, keepdims=True)

    for block in range(blocks):
        pieces = block_inputs((means, log_scales, rotations, logits, coefs), block, views)
        _, pull = jax.vjp(lambda *own: project(*own, cam), *pieces)
        seeds = [
            back_ref[pl.ds(block * FEAT + feat, views, stride=blocks * FEAT), :] for feat in range(FEAT)
        ]
        g_means, g_scales, g_rot, g_logit, g_coef = pull(seeds)
        for ref, rows in ((o_means, g_means), (o_scales, g_scales), (o_rot, g_rot), (o_logit, [g_logit]), (o_coef, g_coef)):
            for row, value in enumerate(rows):
                ref[block, pl.ds(row, 1), :] = total(value)


def gather_kernel(picks, src_ref, out_ref):
    renderers, cap = picks.shape
    for r in range(renderers):
        for c in range(cap):
            pick = jnp.maximum(picks[r, c], 0)
            out_ref[pl.ds((r * cap + c) * FEAT, FEAT), :] = src_ref[pl.ds(pick * FEAT, FEAT), :]


def scatter_kernel(picks, src_ref, out_ref, expo_ref):
    renderers, cap = picks.shape
    stride = cap * FEAT + 1
    out_ref[...] = jnp.zeros(out_ref.shape, F32)
    for r in range(renderers):
        for c in range(cap):
            pick = jnp.maximum(picks[r, c], 0)
            place = pl.ds(pick * FEAT, FEAT)
            out_ref[place, :] = out_ref[place, :] + src_ref[pl.ds(r * stride + c * FEAT, FEAT), :]
    terms = src_ref[pl.ds(stride - 1, renderers, stride=stride), :]
    expo_ref[...] = jnp.sum(terms, axis=0, keepdims=True)[:, 0:12]


def split2(value):
    high = value.astype(BF16)
    low = (value - high.astype(F32)).astype(BF16)
    return high, low


def monomials(part, pixel):
    spot_x = (pixel % 16).astype(F32) - 7.5
    spot_y = (pixel // 16).astype(F32) - 7.5
    value = jnp.where(part == 0, 1.0, 0.0)
    value = jnp.where(part == 1, spot_x, value)
    value = jnp.where(part == 2, spot_y, value)
    value = jnp.where(part == 3, spot_x * spot_x, value)
    value = jnp.where(part == 4, spot_x * spot_y, value)
    return jnp.where(part == 5, spot_y * spot_y, value)


def dot(left, right):
    return jnp.dot(left, right, preferred_element_type=F32)


def render_kernel(
    tile_ids,
    slots,
    expo,
    in_ref,
    goal_ref,
    shown_ref,
    grad_ref,
    raw,
    mat,
    mat_h,
    mat_m,
    left,
    mono,
    mono_t,
    al0,
    al1,
    wt0,
    wt1,
    gm0,
    gm1,
    wt_h,
    wt_l,
    ccol,
    gall,
    gsplit,
    gtr,
):
    tiles, kmax = slots.shape
    groups = tiles // 8
    picks = tiles * kmax
    cap = 2
    stride = cap * FEAT + 1
    scene = grad_ref.shape[0] // stride
    rows16 = lax.broadcasted_iota(jnp.int32, (16, G), 0)
    lanes = lax.broadcasted_iota(jnp.int32, (1, G), 1)
    alphas, weights, slopes = (al0, al1), (wt0, wt1), (gm0, gm1)

    part = lax.broadcasted_iota(jnp.int32, (G, PIX), 0) % 16
    pixel = lax.broadcasted_iota(jnp.int32, (G, PIX), 1)
    table = monomials(part, pixel).astype(BF16)
    for piece in range(3):
        mono[piece * G : (piece + 1) * G, :] = table
    part_t = lax.broadcasted_iota(jnp.int32, (PIX, G), 1) % 16
    pixel_t = lax.broadcasted_iota(jnp.int32, (PIX, G), 0)
    table_t = monomials(part_t, pixel_t).astype(BF16)
    mono_t[0:PIX, :] = table_t
    mono_t[PIX : 2 * PIX, :] = table_t

    def place(group, k, t):
        return (group * kmax + k) * 8 + t

    for group in range(groups):
        for t in range(8):
            tile = group * 8 + t
            tile_id = tile_ids[tile]
            mid_x = ((tile_id % TILE_COLS) * 16 + 8).astype(F32)
            mid_y = ((tile_id // TILE_COLS) * 16 + 8).astype(F32)
            shift = jnp.where(rows16 == 0, mid_x, jnp.where(rows16 == 1, mid_y, 0.0))
            for k in range(kmax):
                slot = slots[tile, k]
                base = jnp.maximum(slot, 0) * FEAT
                spot = place(group, k, t) * 16
                raw[spot : spot + FEAT, :] = in_ref[pl.ds(base, FEAT), :] - shift[0:FEAT]
                raw[spot + FEAT : spot + FEAT + 1, :] = jnp.full((1, G), jnp.where(slot < 0, -4000.0, 0.0))

    def feature(index):
        return raw[pl.ds(index, picks, stride=16), :]

    off_x, off_y, con_a, con_b, con_c, opac = [feature(i) for i in range(6)]
    poly_a = con_a * (-0.5 * LOG2E)
    poly_b = con_b * (-LOG2E)
    poly_c = con_c * (-0.5 * LOG2E)
    lead = poly_a * off_x + poly_b * off_y
    tail = poly_c * off_y
    coefs = [
        off_x * lead + off_y * tail + jnp.log(opac) * LOG2E + feature(FEAT),
        -(lead + poly_a * off_x),
        -(2.0 * tail + poly_b * off_x),
        poly_a,
        poly_b,
        poly_c,
    ]
    mat[...] = jnp.zeros(mat.shape, F32)
    for index in range(6):
        mat[pl.ds(index, picks, stride=16), :] = coefs[index]
    for channel in range(3):
        mat[pl.ds(8 + channel, picks, stride=16), :] = feature(6 + channel)
    whole = mat[...]
    high, low = split2(whole)
    mat_h[...] = high
    mat_m[...] = low

    for group in range(groups):
        for k in range(kmax):
            chunk = group * kmax + k
            turned = mat[chunk * G : (chunk + 1) * G, :].T
            first = turned.astype(BF16)
            rest = turned - first.astype(F32)
            second = rest.astype(BF16)
            third = (rest - second.astype(F32)).astype(BF16)
            trio = jnp.concatenate([first, second, third], axis=1)
            left[chunk * G : (chunk + 1) * G, :] = trio
            lanes3 = lax.broadcasted_iota(jnp.int32, (1, 3 * G), 1) % G
            for t in range(8):
                mask = jnp.where(lanes3 // 16 == t, 1.0, 0.0).astype(BF16)
                alpha = jnp.exp2(dot(trio * mask, mono[...]))
                for half in range(2):
                    alphas[half][pl.ds(chunk * G * 8 + t, G, stride=8), :] = alpha[:, half * G : (half + 1) * G]

    count = kmax * G

    def forward(step, keeps):
        keeps = list(keeps)
        for group in range(groups):
            row = pl.multiple_of((group * count + step) * 8, 8)
            for half in range(2):
                at = group * 2 + half
                weight = keeps[at] * alphas[half][pl.ds(row, 8), :]
                weights[half][pl.ds(row, 8), :] = weight
                keeps[at] = keeps[at] - weight
        return tuple(keeps)

    ones = jnp.ones((8, G), F32)
    lax.fori_loop(0, count, forward, (ones,) * (2 * groups), unroll=8)

    for group in range(groups):
        for t in range(8):
            total = jnp.zeros((16, PIX), F32)
            for k in range(kmax):
                spot = place(group, k, t)
                rows = pl.ds((group * kmax + k) * G * 8 + t, G, stride=8)
                weight = jnp.concatenate([weights[0][rows, :], weights[1][rows, :]], axis=1)
                w_high, w_low = split2(weight)
                wt_h[spot * G : (spot + 1) * G, :] = w_high
                wt_l[spot * G : (spot + 1) * G, :] = w_low
                m_high = mat_h[spot * 16 : spot * 16 + 16, :]
                m_low = mat_m[spot * 16 : spot * 16 + 16, :]
                both = dot(jnp.concatenate([m_high, m_low], axis=0), w_high)
                total = total + both[0:16] + both[16:32] + dot(m_high, w_low)
            for channel in range(3):
                row = channel * tiles + group * 8 + t
                ccol[row : row + 1, :] = total[8 + channel : 9 + channel, :]

    colour = [ccol[c * tiles : (c + 1) * tiles, :] for c in range(3)]
    miss = []
    for i in range(3):
        value = colour[i] + expo[0, 9 + i]
        for j in range(3):
            value = value + expo[0, 3 * i + j] * colour[j]
        shown_ref[:, i, :] = value
        miss.append(value - goal_ref[:, i, :])
    slope = []
    for j in range(3):
        value = miss[j]
        for i in range(3):
            value = value + expo[0, 3 * i + j] * miss[i]
        slope.append(value)
    terms = [miss[i] * colour[j] for i in range(3) for j in range(3)] + miss
    expo_row = jnp.zeros((1, G), F32)
    for index, value in enumerate(terms):
        folded = jnp.sum(value[:, 0:G] + value[:, G : 2 * G], axis=0, keepdims=True)
        expo_row = jnp.where(lanes == index, jnp.sum(folded, axis=1, keepdims=True), expo_row)

    for group in range(groups):
        base = group * 3 * G
        for half in range(2):
            side = slice(half * G, (half + 1) * G)
            highs, lows = [], []
            for channel in range(3):
                value = slope[channel][group * 8 : group * 8 + 8, side]
                s_high = value.astype(BF16).astype(F32)
                highs.append(s_high)
                lows.append(value - s_high)
            gall[...] = jnp.zeros(gall.shape, F32)
            for channel in range(3):
                gall[pl.ds(8 + channel, 8, stride=16), :] = lows[channel]
            gsplit[base + 2 * G : base + 3 * G, side] = gall[...].astype(BF16)
            for channel in range(3):
                gall[pl.ds(8 + channel, 8, stride=16), :] = highs[channel]
            g_high = gall[...].astype(BF16)
            gsplit[base : base + G, side] = g_high
            gsplit[base + G : base + 2 * G, side] = g_high
            for channel in range(3):
                gall[pl.ds(11 + channel, 8, stride=16), :] = lows[channel]
            turned = gall[...].T.astype(BF16)
            start = group * 2 * PIX + half * G
            gtr[start : start + G, :] = turned
            gtr[start + PIX : start + PIX + G, :] = turned
        g_rhs = gsplit[base : base + 3 * G, :]
        for k in range(kmax):
            chunk = group * kmax + k
            first = left[chunk * G : (chunk + 1) * G, 0:G]
            second = left[chunk * G : (chunk + 1) * G, G : 2 * G]
            trio = jnp.concatenate([first, second, first], axis=1)
            lanes3 = lax.broadcasted_iota(jnp.int32, (1, 3 * G), 1) % G
            for t in range(8):
                mask = jnp.where(lanes3 // 16 == t, 1.0, 0.0).astype(BF16)
                value = dot(trio * mask, g_rhs)
                for half in range(2):
                    slopes[half][pl.ds(chunk * G * 8 + t, G, stride=8), :] = value[:, half * G : (half + 1) * G]

    def backward(step, behind):
        behind = list(behind)
        for group in range(groups):
            row = pl.multiple_of((group * count + (count - 1 - step)) * 8, 8)
            for half in range(2):
                at = group * 2 + half
                gap = slopes[half][pl.ds(row, 8), :] - behind[at]
                slopes[half][pl.ds(row, 8), :] = weights[half][pl.ds(row, 8), :] * gap
                behind[at] = behind[at] + alphas[half][pl.ds(row, 8), :] * gap
        return tuple(behind)

    zeros = jnp.zeros((8, G), F32)
    lax.fori_loop(0, count, backward, (zeros,) * (2 * groups), unroll=8)

    lane_tile = lax.broadcasted_iota(jnp.int32, (G, G), 1) // 16
    for group in range(groups):
        g_t = gtr[group * 2 * PIX : (group + 1) * 2 * PIX, :]
        for k in range(kmax):
            chunk = group * kmax + k
            acc = jnp.zeros((G, G), F32)
            for t in range(8):
                spot = place(group, k, t)
                rows = pl.ds(chunk * G * 8 + t, G, stride=8)
                value = jnp.concatenate([slopes[0][rows, :], slopes[1][rows, :]], axis=1)
                v_high, v_low = split2(value)
                out = dot(jnp.concatenate([v_high, v_low], axis=1), mono_t[...])
                w_high = wt_h[spot * G : (spot + 1) * G, :]
                w_low = wt_l[spot * G : (spot + 1) * G, :]
                out = out + dot(jnp.concatenate([w_high, w_low], axis=1), g_t)
                acc = jnp.where(lane_tile == t, out, acc)
            mat[chunk * G : (chunk + 1) * G, :] = acc.T

    def moment(index):
        return mat[pl.ds(index, picks, stride=16), :]

    sum_0, sum_x, sum_y, sum_xx, sum_xy, sum_yy = [moment(i) for i in range(6)]
    off_x, off_y, con_a, con_b, con_c, opac = [feature(i) for i in range(6)]
    cen_x = sum_x - off_x * sum_0
    cen_y = sum_y - off_y * sum_0
    cen_xx = sum_xx - off_x * (sum_x + cen_x)
    cen_yy = sum_yy - off_y * (sum_y + cen_y)
    cen_xy = sum_xy - off_x * sum_y - off_y * cen_x
    outs = [
        con_a * cen_x + con_b * cen_y,
        con_b * cen_x + con_c * cen_y,
        -0.5 * cen_xx,
        -cen_xy,
        -0.5 * cen_yy,
        sum_0 / opac,
    ] + [moment(8 + c) + moment(11 + c) for c in range(3)]
    for index, value in enumerate(outs):
        raw[pl.ds(index, picks, stride=16), :] = value

    grad_ref[...] = jnp.zeros(grad_ref.shape, F32)
    for group in range(groups):
        for k in range(kmax):
            for t in range(8):
                slot = jnp.maximum(slots[group * 8 + t, k], 0)
                where = pl.ds((slot // cap) * stride + (slot % cap) * FEAT, FEAT)
                spot = place(group, k, t) * 16
                grad_ref[where, :] = grad_ref[where, :] + raw[spot : spot + FEAT, :]
    grad_ref[pl.ds(stride - 1, scene, stride=stride), :] = jnp.broadcast_to(expo_row, (scene, G))


def vmem():
    return pl.BlockSpec(memory_space=pltpu.VMEM)


def smem():
    return pl.BlockSpec(memory_space=pltpu.SMEM)


def across(rows, axis, parts):
    shaped = rows.reshape(parts, rows.shape[0] // parts, 1, G)
    moved = lax.all_to_all(shaped, axis, split_axis=0, concat_axis=0, tiled=True)
    return moved.reshape(rows.shape)


def render(tile_ids, slots, expo, incoming, goal, interpret=False):
    tiles, kmax = slots.shape
    picks = tiles * kmax
    groups = tiles // 8
    scene = incoming.shape[0] // (2 * FEAT)
    big = pltpu.VMEM((picks * G, G), F32)
    return pl.pallas_call(
        render_kernel,
        out_shape=(
            jax.ShapeDtypeStruct((tiles, 3, PIX), F32),
            jax.ShapeDtypeStruct((scene * (2 * FEAT + 1), G), F32),
        ),
        in_specs=[smem(), smem(), smem(), vmem(), vmem()],
        out_specs=(vmem(), vmem()),
        scratch_shapes=[
            pltpu.VMEM((picks * 16, G), F32),
            pltpu.VMEM((picks * 16, G), F32),
            pltpu.VMEM((picks * 16, G), BF16),
            pltpu.VMEM((picks * 16, G), BF16),
            pltpu.VMEM((groups * kmax * G, 3 * G), BF16),
            pltpu.VMEM((3 * G, PIX), BF16),
            pltpu.VMEM((2 * PIX, G), BF16),
            big,
            big,
            big,
            big,
            big,
            big,
            pltpu.VMEM((picks * G, PIX), BF16),
            pltpu.VMEM((picks * G, PIX), BF16),
            pltpu.VMEM((3 * tiles, PIX), F32),
            pltpu.VMEM((G, G), F32),
            pltpu.VMEM((groups * 3 * G, PIX), BF16),
            pltpu.VMEM((groups * 2 * PIX, G), BF16),
        ],
        compiler_params=pltpu.CompilerParams(vmem_limit_bytes=56 * 1024 * 1024),
        name="render",
        interpret=interpret,
    )(tile_ids, slots, expo, incoming, goal)


def local(
    means,
    log_scales,
    rotations,
    opacity_logits,
    colour_coefs,
    cameras,
    exposure,
    target,
    tile_ids,
    send_list,
    pair_slots,
):
    views = lax.axis_size("view")
    scene = lax.axis_size("scene")
    blocks = means.shape[0]
    cap = send_list.shape[3]
    pieces = (means, log_scales, rotations, opacity_logits, colour_coefs)
    picks = send_list[0, 0]
    own_rows = jax.ShapeDtypeStruct((views * blocks * FEAT, G), F32)
    own_proj = pl.pallas_call(
        project_kernel,
        out_shape=own_rows,
        in_specs=[vmem()] * 6,
        out_specs=vmem(),
        name="project",
    )(*pieces, cameras)
    projected = across(own_proj, "view", views)
    outgoing = pl.pallas_call(
        gather_kernel,
        out_shape=jax.ShapeDtypeStruct((scene * cap * FEAT, G), F32),
        in_specs=[smem(), vmem()],
        out_specs=vmem(),
        name="gather",
    )(picks, projected)
    incoming = across(outgoing, "scene", scene)
    shown, grad_rows = render(tile_ids[0], pair_slots[0], exposure, incoming, target[0])
    returned = across(grad_rows, "scene", scene)
    grad_proj, grad_expo = pl.pallas_call(
        scatter_kernel,
        out_shape=(own_rows, jax.ShapeDtypeStruct((1, 12), F32)),
        in_specs=[smem(), vmem()],
        out_specs=(vmem(), vmem()),
        name="scatter",
    )(picks, returned)
    sent_back = across(grad_proj, "view", views)
    grads = pl.pallas_call(
        unproject_kernel,
        out_shape=tuple(jax.ShapeDtypeStruct(piece.shape, F32) for piece in pieces),
        in_specs=[vmem()] * 7,
        out_specs=tuple(vmem() for _ in pieces),
        name="unproject",
    )(*pieces, cameras, sent_back)
    return (shown[None], *grads, grad_expo)


def solution(mesh):
    return jax.shard_map(
        local,
        mesh=mesh,
        in_specs=(
            P(("view", "scene"), None, None),
            P(("view", "scene"), None, None),
            P(("view", "scene"), None, None),
            P(("view", "scene"), None, None),
            P(("view", "scene"), None, None),
            P(),
            P("view", None),
            P("view", "scene", None, None),
            P("view", "scene"),
            P("view", "scene", None, None),
            P("view", "scene", None),
        ),
        out_specs=(
            P("view", "scene", None, None),
            P(("view", "scene"), None, None),
            P(("view", "scene"), None, None),
            P(("view", "scene"), None, None),
            P(("view", "scene"), None, None),
            P(("view", "scene"), None, None),
            P("view", None),
        ),
        check_vma=False,
    )
```

```python
import jax
import jax.numpy as jnp
from jax import lax
from jax.experimental import pallas as pl
from jax.experimental.pallas import tpu as pltpu
from jax.sharding import PartitionSpec as P

PIX = 256
TILE_COLS = 32
G = 128
FEAT = 9
F32 = jnp.float32
BF16 = jnp.bfloat16
LOG2E = 1.4426950408889634

SH_ZERO = 0.28209479177387814
SH_ONE = 0.4886025119029199
SH_TWO = (
    1.0925484305920792,
    -1.0925484305920792,
    0.31539156525252005,
    -1.0925484305920792,
    0.5462742152960396,
)
SH_THREE = (
    -0.5900435899266435,
    2.890611442640554,
    -0.4570457994644658,
    0.3731763325901154,
    -0.4570457994644658,
    1.445305721320277,
    -0.5900435899266435,
)


def harmonics(dir_x, dir_y, dir_z):
    sq_x, sq_y, sq_z = (dir_x * dir_x, dir_y * dir_y, dir_z * dir_z)
    return [
        SH_ZERO * jnp.ones_like(dir_x),
        -SH_ONE * dir_y,
        SH_ONE * dir_z,
        -SH_ONE * dir_x,
        SH_TWO[0] * dir_x * dir_y,
        SH_TWO[1] * dir_y * dir_z,
        SH_TWO[2] * (2.0 * sq_z - sq_x - sq_y),
        SH_TWO[3] * dir_x * dir_z,
        SH_TWO[4] * (sq_x - sq_y),
        SH_THREE[0] * dir_y * (3.0 * sq_x - sq_y),
        SH_THREE[1] * dir_x * dir_y * dir_z,
        SH_THREE[2] * dir_y * (4.0 * sq_z - sq_x - sq_y),
        SH_THREE[3] * dir_z * (2.0 * sq_z - 3.0 * sq_x - 3.0 * sq_y),
        SH_THREE[4] * dir_x * (4.0 * sq_z - sq_x - sq_y),
        SH_THREE[5] * dir_z * (sq_x - sq_y),
        SH_THREE[6] * dir_x * (sq_x - 3.0 * sq_y),
    ]


def project(position, log_scales, quats, logit, coefs, cam):
    rotation = [[cam[3 * row + col] for col in range(3)] for row in range(3)]
    translation = cam[9:12]
    focal_x, focal_y, centre_x, centre_y = cam[12:16]
    view_pos = [
        rotation[row][0] * position[0]
        + rotation[row][1] * position[1]
        + rotation[row][2] * position[2]
        + translation[row]
        for row in range(3)
    ]
    inv_depth = 1.0 / view_pos[2]
    quat_w = quats[0] + 3.0
    quat_x, quat_y, quat_z = quats[1:4]
    quat_norm = jnp.sqrt(quat_w * quat_w + quat_x * quat_x + quat_y * quat_y + quat_z * quat_z)
    inv_norm = 1.0 / quat_norm
    quat_w, quat_x, quat_y, quat_z = (
        quat_w * inv_norm,
        quat_x * inv_norm,
        quat_y * inv_norm,
        quat_z * inv_norm,
    )
    spin = [
        [
            1.0 - 2.0 * (quat_y * quat_y + quat_z * quat_z),
            2.0 * (quat_x * quat_y - quat_w * quat_z),
            2.0 * (quat_x * quat_z + quat_w * quat_y),
        ],
        [
            2.0 * (quat_x * quat_y + quat_w * quat_z),
            1.0 - 2.0 * (quat_x * quat_x + quat_z * quat_z),
            2.0 * (quat_y * quat_z - quat_w * quat_x),
        ],
        [
            2.0 * (quat_x * quat_z - quat_w * quat_y),
            2.0 * (quat_y * quat_z + quat_w * quat_x),
            1.0 - 2.0 * (quat_x * quat_x + quat_y * quat_y),
        ],
    ]
    scales = [jnp.exp(row) for row in log_scales]
    world = [[spin[row][col] * scales[col] for col in range(3)] for row in range(3)]
    step_x = focal_x * inv_depth
    step_y = focal_y * inv_depth
    slide_x = step_x * view_pos[0] * inv_depth
    slide_y = step_y * view_pos[1] * inv_depth
    jac = [
        [step_x * rotation[0][col] - slide_x * rotation[2][col] for col in range(3)],
        [step_y * rotation[1][col] - slide_y * rotation[2][col] for col in range(3)],
    ]
    screen = [
        [
            jac[row][0] * world[0][col] + jac[row][1] * world[1][col] + jac[row][2] * world[2][col]
            for col in range(3)
        ]
        for row in range(2)
    ]
    sigma_xx = screen[0][0] * screen[0][0] + screen[0][1] * screen[0][1] + screen[0][2] * screen[0][2] + 0.3
    sigma_yy = screen[1][0] * screen[1][0] + screen[1][1] * screen[1][1] + screen[1][2] * screen[1][2] + 0.3
    sigma_xy = screen[0][0] * screen[1][0] + screen[0][1] * screen[1][1] + screen[0][2] * screen[1][2]
    inv_det = 1.0 / (sigma_xx * sigma_yy - sigma_xy * sigma_xy)
    screen_x = step_x * view_pos[0] + centre_x
    screen_y = step_y * view_pos[1] + centre_y
    opacity = 1.0 / (1.0 + jnp.exp(-logit))
    eye = [
        -(
            rotation[0][col] * translation[0]
            + rotation[1][col] * translation[1]
            + rotation[2][col] * translation[2]
        )
        for col in range(3)
    ]
    offs = [position[col] - eye[col] for col in range(3)]
    inv_dist = 1.0 / jnp.sqrt(offs[0] * offs[0] + offs[1] * offs[1] + offs[2] * offs[2])
    basis = harmonics(offs[0] * inv_dist, offs[1] * inv_dist, offs[2] * inv_dist)
    colours = []
    for channel in range(3):
        total = basis[0] * coefs[channel]
        for band in range(1, 16):
            total = total + basis[band] * coefs[3 * band + channel]
        colours.append(jnp.maximum(0.5 + total, 0.0))
    return [
        screen_x,
        screen_y,
        sigma_yy * inv_det,
        -sigma_xy * inv_det,
        sigma_xx * inv_det,
        opacity,
    ] + colours


def block_inputs(refs, block, views):
    means, log_scales, rotations, logits, coefs = refs

    def rows(ref, count):
        return [jnp.broadcast_to(ref[block, pl.ds(r, 1), :], (views, G)) for r in range(count)]

    def turned(ref):
        return [jnp.broadcast_to(ref[r, pl.ds(block, 1), :], (views, G)) for r in range(3)]

    return (turned(means), turned(log_scales), rows(rotations, 4), rows(logits, 1)[0], rows(coefs, 48))


def camera_columns(cam_ref, views):
    cams = cam_ref[...]
    return [jnp.broadcast_to(cams[:, col : col + 1], (views, G)) for col in range(16)]


def project_kernel(means, log_scales, rotations, logits, coefs, cam_ref, out_ref):
    views = cam_ref.shape[0]
    blocks = rotations.shape[0]
    cam = camera_columns(cam_ref, views)
    for block in range(blocks):
        pieces = block_inputs((means, log_scales, rotations, logits, coefs), block, views)
        for feat, value in enumerate(project(*pieces, cam)):
            out_ref[pl.ds(block * FEAT + feat, views, stride=blocks * FEAT), :] = value


def unproject_kernel(
    means, log_scales, rotations, logits, coefs, cam_ref, back_ref, o_means, o_scales, o_rot, o_logit, o_coef
):
    views = cam_ref.shape[0]
    blocks = rotations.shape[0]
    cam = camera_columns(cam_ref, views)

    def total(value):
        return jnp.sum(value, axis=0, keepdims=True)

    for block in range(blocks):
        pieces = block_inputs((means, log_scales, rotations, logits, coefs), block, views)
        _, pull = jax.vjp(lambda *own: project(*own, cam), *pieces)
        seeds = [
            back_ref[pl.ds(block * FEAT + feat, views, stride=blocks * FEAT), :] for feat in range(FEAT)
        ]
        g_means, g_scales, g_rot, g_logit, g_coef = pull(seeds)
        for ref, rows in ((o_means, g_means), (o_scales, g_scales)):
            for row, value in enumerate(rows):
                ref[row, pl.ds(block, 1), :] = total(value)
        for ref, rows in ((o_rot, g_rot), (o_logit, [g_logit]), (o_coef, g_coef)):
            for row, value in enumerate(rows):
                ref[block, pl.ds(row, 1), :] = total(value)


def gather_kernel(picks, src_ref, out_ref):
    cap, renderers = picks.shape
    for r in range(renderers):
        for c in range(cap):
            pick = jnp.maximum(picks[c, r], 0)
            out_ref[pl.ds((r * cap + c) * FEAT, FEAT), :] = src_ref[pl.ds(pick * FEAT, FEAT), :]


def scatter_kernel(picks, src_ref, out_ref, expo_ref):
    cap, renderers = picks.shape
    stride = cap * FEAT + 1
    out_ref[...] = jnp.zeros(out_ref.shape, F32)
    for r in range(renderers):
        for c in range(cap):
            pick = jnp.maximum(picks[c, r], 0)
            place = pl.ds(pick * FEAT, FEAT)
            out_ref[place, :] = out_ref[place, :] + src_ref[pl.ds(r * stride + c * FEAT, FEAT), :]
    terms = src_ref[pl.ds(stride - 1, renderers, stride=stride), :]
    expo_ref[...] = jnp.sum(terms, axis=0, keepdims=True)[:, 0:12]


def split2(value):
    high = value.astype(BF16)
    low = (value - high.astype(F32)).astype(BF16)
    return high, low


def pieces3(value):
    high = value.astype(BF16).astype(F32)
    rest = value - high
    middle = rest.astype(BF16).astype(F32)
    return high, middle, rest - middle


def monomials(part, pixel):
    spot_x = (pixel % 16).astype(F32) - 7.5
    spot_y = (pixel // 16).astype(F32) - 7.5
    value = jnp.where(part == 0, 1.0, 0.0)
    value = jnp.where(part == 1, spot_x, value)
    value = jnp.where(part == 2, spot_y, value)
    value = jnp.where(part == 3, spot_x * spot_x, value)
    value = jnp.where(part == 4, spot_x * spot_y, value)
    return jnp.where(part == 5, spot_y * spot_y, value)


def dot(left, right):
    return jnp.dot(left, right, preferred_element_type=F32)


def dot_t(left, right):
    return lax.dot_general(left, right, (((1,), (1,)), ((), ())), preferred_element_type=F32)


ROWS = 32


def render_kernel(
    tile_ids,
    slots,
    expo,
    in_ref,
    goal_ref,
    shown_ref,
    grad_ref,
    raw,
    mat,
    mat_c,
    mat_b,
    left,
    mono,
    mono_t,
    al0,
    al1,
    wt0,
    wt1,
    gm0,
    gm1,
    hh0,
    hh1,
    wt_h,
    wt_l,
    ccol,
    gall,
    g_rhs,
    g_own,
    mom,
):
    kmax, tiles = slots.shape
    groups = tiles // 8
    picks = tiles * kmax
    cap = 2
    stride = cap * FEAT + 1
    scene = grad_ref.shape[0] // stride
    wide = 8 * ROWS
    rows16 = lax.broadcasted_iota(jnp.int32, (16, G), 0)
    lanes = lax.broadcasted_iota(jnp.int32, (1, G), 1)
    alphas, weights, slopes, moved = (al0, al1), (wt0, wt1), (gm0, gm1), (hh0, hh1)

    row = lax.broadcasted_iota(jnp.int32, (wide, PIX), 0) // 8
    part = jnp.where(row < 18, row % 6, 6)
    mono[...] = monomials(part, lax.broadcasted_iota(jnp.int32, (wide, PIX), 1)).astype(BF16)
    part = lax.broadcasted_iota(jnp.int32, (16, PIX), 0)
    mono_t[...] = monomials(part, lax.broadcasted_iota(jnp.int32, (16, PIX), 1)).astype(BF16)

    def place(group, k, t):
        return (group * kmax + k) * 8 + t

    for group in range(groups):
        for t in range(8):
            tile = group * 8 + t
            tile_id = tile_ids[tile]
            mid_x = ((tile_id % TILE_COLS) * 16 + 8).astype(F32)
            mid_y = ((tile_id // TILE_COLS) * 16 + 8).astype(F32)
            shift = jnp.where(rows16 == 0, mid_x, jnp.where(rows16 == 1, mid_y, 0.0))
            for k in range(kmax):
                slot = slots[k, tile]
                base = jnp.maximum(slot, 0) * FEAT
                spot = place(group, k, t) * 16
                raw[spot : spot + FEAT, :] = in_ref[pl.ds(base, FEAT), :] - shift[0:FEAT]
                raw[spot + FEAT : spot + FEAT + 1, :] = jnp.full((1, G), jnp.where(slot < 0, -4000.0, 0.0))

    def feature(index):
        return raw[pl.ds(index, picks, stride=16), :]

    off_x, off_y, con_a, con_b, con_c, opac = [feature(i) for i in range(6)]
    poly_a = con_a * (-0.5 * LOG2E)
    poly_b = con_b * (-LOG2E)
    poly_c = con_c * (-0.5 * LOG2E)
    lead = poly_a * off_x + poly_b * off_y
    tail = poly_c * off_y
    coefs = [
        off_x * lead + off_y * tail + jnp.log(opac) * LOG2E + feature(FEAT),
        -(lead + poly_a * off_x),
        -(2.0 * tail + poly_b * off_x),
        poly_a,
        poly_b,
        poly_c,
    ]
    blank = jnp.zeros((8, G), F32)
    rows_of = [blank] * ROWS
    for index in range(6):
        for piece, value in enumerate(pieces3(coefs[index])):
            rows_of[6 * piece + index] = value
    mat_c[...] = jnp.zeros(mat_c.shape, F32)
    for channel in range(3):
        high, middle, _ = pieces3(feature(6 + channel))
        rows_of[18 + channel] = high
        rows_of[21 + channel] = middle
        rows_of[24 + channel] = high
        mat_c[pl.ds(channel, picks, stride=16), :] = high
        mat_c[pl.ds(3 + channel, picks, stride=16), :] = middle
    for chunk in range(groups * kmax):
        for index, value in enumerate(rows_of):
            start = chunk * wide + index * 8
            mat[start : start + 8, :] = value if index >= 27 else value[chunk * 8 : chunk * 8 + 8]
    mat_b[...] = mat_c[...].astype(BF16)

    lane_tile = lax.broadcasted_iota(jnp.int32, (1, wide), 1) % 8
    masks = [jnp.where(lane_tile == t, 1.0, 0.0).astype(BF16) for t in range(8)]

    for chunk in range(groups * kmax):
        sides = [mat[chunk * wide + half * G : chunk * wide + (half + 1) * G, :].T for half in range(2)]
        turned = jnp.concatenate(sides, axis=1).astype(BF16)
        left[chunk * G : (chunk + 1) * G, :] = turned
        for t in range(8):
            alpha = jnp.exp2(dot(turned * masks[t], mono[...]))
            for half in range(2):
                alphas[half][pl.ds(chunk * G * 8 + t, G, stride=8), :] = alpha[:, half * G : (half + 1) * G]

    count = kmax * G

    def forward(step, keeps):
        keeps = list(keeps)
        for group in range(groups):
            row = pl.multiple_of((group * count + step) * 8, 8)
            for half in range(2):
                at = group * 2 + half
                alpha = alphas[half][pl.ds(row, 8), :]
                weights[half][pl.ds(row, 8), :] = keeps[at] * alpha
                keeps[at] = keeps[at] * (1.0 - alpha)
        return tuple(keeps)

    ones = jnp.ones((8, G), F32)
    lax.fori_loop(0, count, forward, (ones,) * (2 * groups), unroll=8)

    for group in range(groups):
        for t in range(8):
            total = jnp.zeros((16, PIX), F32)
            for k in range(kmax):
                spot = place(group, k, t)
                rows = pl.ds((group * kmax + k) * G * 8 + t, G, stride=8)
                weight = jnp.concatenate([weights[0][rows, :], weights[1][rows, :]], axis=1)
                w_high, w_low = split2(weight)
                wt_h[spot * G : (spot + 1) * G, :] = w_high
                wt_l[spot * G : (spot + 1) * G, :] = w_low
                own = mat_b[spot * 16 : (spot + 1) * 16, :]
                total = total + dot(own, w_high) + dot(own, w_low)
            for channel in range(3):
                row = channel * tiles + group * 8 + t
                ccol[row : row + 1, :] = total[channel : channel + 1, :] + total[3 + channel : 4 + channel, :]

    colour = [ccol[c * tiles : (c + 1) * tiles, :] for c in range(3)]
    miss = []
    for i in range(3):
        value = colour[i] + expo[0, 9 + i]
        for j in range(3):
            value = value + expo[0, 3 * i + j] * colour[j]
        shown_ref[i] = value
        miss.append(value - goal_ref[i])
    slope = []
    for j in range(3):
        value = miss[j]
        for i in range(3):
            value = value + expo[0, 3 * i + j] * miss[i]
        slope.append(value)
    terms = [miss[i] * colour[j] for i in range(3) for j in range(3)] + miss
    expo_row = jnp.zeros((1, G), F32)
    for index, value in enumerate(terms):
        folded = jnp.sum(value[:, 0:G] + value[:, G : 2 * G], axis=0, keepdims=True)
        expo_row = jnp.where(lanes == index, jnp.sum(folded, axis=1, keepdims=True), expo_row)

    highs = [value.astype(BF16).astype(F32) for value in slope]
    lows = [value - high for value, high in zip(slope, highs)]
    for group in range(groups):
        span = slice(group * 8, group * 8 + 8)
        nine = [value[span] for value in highs + highs + lows]
        stack = [jnp.zeros((18 * 8, PIX), F32)] + nine + [jnp.zeros(((ROWS - 27) * 8, PIX), F32)]
        g_rhs[group * wide : (group + 1) * wide, :] = jnp.concatenate(stack, axis=0).astype(BF16)
    gall[...] = jnp.zeros(gall.shape, F32)
    for half in range(2):
        side = slice(half * G, (half + 1) * G)
        for channel in range(3):
            gall[pl.ds(channel, tiles, stride=16), :] = highs[channel][:, side]
            gall[pl.ds(3 + channel, tiles, stride=16), :] = lows[channel][:, side]
        g_own[:, side] = gall[...].astype(BF16)
    for chunk in range(groups * kmax):
        turned = left[chunk * G : (chunk + 1) * G, :]
        group = chunk // kmax
        right = g_rhs[group * wide : (group + 1) * wide, :]
        for t in range(8):
            value = dot(turned * masks[t], right)
            for half in range(2):
                slopes[half][pl.ds(chunk * G * 8 + t, G, stride=8), :] = value[:, half * G : (half + 1) * G]

    batch = 8

    def backward(step, behind):
        behind = list(behind)
        base = pl.multiple_of((count - batch - step * batch) * 8, 8 * batch)
        for inner in range(batch - 1, -1, -1):
            for group in range(groups):
                rows = pl.ds(base + (group * count + inner) * 8, 8)
                for half in range(2):
                    at = group * 2 + half
                    alpha = alphas[half][rows, :]
                    value = slopes[half][rows, :]
                    moved[half][rows, :] = weights[half][rows, :] * (value - behind[at])
                    behind[at] = behind[at] * (1.0 - alpha) + alpha * value
        return tuple(behind)

    zeros = jnp.zeros((8, G), F32)
    lax.fori_loop(0, count // batch, backward, (zeros,) * (2 * groups))

    for group in range(groups):
        for k in range(kmax):
            for t in range(8):
                spot = place(group, k, t)
                rows = pl.ds((group * kmax + k) * G * 8 + t, G, stride=8)
                value = jnp.concatenate([moved[0][rows, :].T, moved[1][rows, :].T], axis=0)
                v_high, v_low = split2(value)
                table = mono_t[...]
                sums = dot(table, v_high) + dot(table, v_low)
                mom[spot * 8 : (spot + 1) * 8, :] = sums[0:8]
                own = g_own[(group * 8 + t) * 16 : (group * 8 + t + 1) * 16, :]
                w_high = wt_h[spot * G : (spot + 1) * G, :]
                w_low = wt_l[spot * G : (spot + 1) * G, :]
                mat_c[spot * 16 : (spot + 1) * 16, :] = dot_t(own, w_high) + dot_t(own, w_low)

    sum_0, sum_x, sum_y, sum_xx, sum_xy, sum_yy = [mom[pl.ds(i, picks, stride=8), :] for i in range(6)]
    off_x, off_y, con_a, con_b, con_c, opac = [feature(i) for i in range(6)]
    cen_x = sum_x - off_x * sum_0
    cen_y = sum_y - off_y * sum_0
    cen_xx = sum_xx - off_x * (sum_x + cen_x)
    cen_yy = sum_yy - off_y * (sum_y + cen_y)
    cen_xy = sum_xy - off_x * sum_y - off_y * cen_x
    outs = [
        con_a * cen_x + con_b * cen_y,
        con_b * cen_x + con_c * cen_y,
        -0.5 * cen_xx,
        -cen_xy,
        -0.5 * cen_yy,
        sum_0 / opac,
    ]
    for channel in range(3):
        outs.append(
            mat_c[pl.ds(channel, picks, stride=16), :] + mat_c[pl.ds(3 + channel, picks, stride=16), :]
        )
    for index, value in enumerate(outs):
        raw[pl.ds(index, picks, stride=16), :] = value

    grad_ref[...] = jnp.zeros(grad_ref.shape, F32)
    for group in range(groups):
        for k in range(kmax):
            for t in range(8):
                slot = jnp.maximum(slots[k, group * 8 + t], 0)
                where = pl.ds((slot // cap) * stride + (slot % cap) * FEAT, FEAT)
                spot = place(group, k, t) * 16
                grad_ref[where, :] = grad_ref[where, :] + raw[spot : spot + FEAT, :]
    grad_ref[pl.ds(stride - 1, scene, stride=stride), :] = jnp.broadcast_to(expo_row, (scene, G))


def vmem():
    return pl.BlockSpec(memory_space=pltpu.VMEM)


def smem():
    return pl.BlockSpec(memory_space=pltpu.SMEM)


def across(rows, axis, parts):
    shaped = rows.reshape(parts, rows.shape[0] // parts, 1, G)
    moved = lax.all_to_all(shaped, axis, split_axis=0, concat_axis=0, tiled=True)
    return moved.reshape(rows.shape)


def near(rows):
    return pltpu.with_memory_space_constraint(rows, pltpu.VMEM)


def render(tile_ids, slots, expo, incoming, goal, interpret=False):
    kmax, tiles = slots.shape
    picks = tiles * kmax
    groups = tiles // 8
    scene = incoming.shape[0] // (2 * FEAT)
    big = pltpu.VMEM((picks * G, G), F32)
    return pl.pallas_call(
        render_kernel,
        out_shape=(
            jax.ShapeDtypeStruct((3, tiles, PIX), F32),
            pltpu.VMEM((scene * (2 * FEAT + 1), G), F32),
        ),
        in_specs=[smem(), smem(), smem(), vmem(), vmem()],
        out_specs=(vmem(), vmem()),
        scratch_shapes=[
            pltpu.VMEM((picks * 16, G), F32),
            pltpu.VMEM((picks * ROWS, G), F32),
            pltpu.VMEM((picks * 16, G), F32),
            pltpu.VMEM((picks * 16, G), BF16),
            pltpu.VMEM((groups * kmax * G, 8 * ROWS), BF16),
            pltpu.VMEM((8 * ROWS, PIX), BF16),
            pltpu.VMEM((16, PIX), BF16),
            big,
            big,
            big,
            big,
            big,
            big,
            big,
            big,
            pltpu.VMEM((picks * G, PIX), BF16),
            pltpu.VMEM((picks * G, PIX), BF16),
            pltpu.VMEM((3 * tiles, PIX), F32),
            pltpu.VMEM((tiles * 16, G), F32),
            pltpu.VMEM((tiles * ROWS, PIX), BF16),
            pltpu.VMEM((tiles * 16, PIX), BF16),
            pltpu.VMEM((picks * 8, G), F32),
        ],
        compiler_params=pltpu.CompilerParams(vmem_limit_bytes=56 * 1024 * 1024),
        name="render",
        interpret=interpret,
    )(tile_ids, slots, expo, incoming, goal)


def local(
    means,
    log_scales,
    rotations,
    opacity_logits,
    colour_coefs,
    cameras,
    exposure,
    target,
    tile_ids,
    send_list,
    pair_slots,
):
    views = lax.axis_size("view")
    scene = lax.axis_size("scene")
    blocks = means.shape[0]
    cap = send_list.shape[3]
    pieces = (
        means.transpose(1, 0, 2),
        log_scales.transpose(1, 0, 2),
        rotations,
        opacity_logits,
        colour_coefs,
    )
    picks = send_list[0, 0].T
    own_count = views * blocks * FEAT
    own_proj = pl.pallas_call(
        project_kernel,
        out_shape=pltpu.VMEM((own_count, G), F32),
        in_specs=[vmem()] * 6,
        out_specs=vmem(),
        name="project",
    )(*pieces, cameras)
    projected = across(own_proj, "view", views)
    outgoing = pl.pallas_call(
        gather_kernel,
        out_shape=pltpu.VMEM((scene * cap * FEAT, G), F32),
        in_specs=[smem(), vmem()],
        out_specs=vmem(),
        name="gather",
    )(picks, near(projected))
    incoming = across(outgoing, "scene", scene)
    shown, grad_rows = render(
        tile_ids[0], pair_slots[0].T, exposure, near(incoming), target[0].transpose(1, 0, 2)
    )
    returned = across(grad_rows, "scene", scene)
    grad_proj, grad_expo = pl.pallas_call(
        scatter_kernel,
        out_shape=(pltpu.VMEM((own_count, G), F32), jax.ShapeDtypeStruct((1, 12), F32)),
        in_specs=[smem(), vmem()],
        out_specs=(vmem(), vmem()),
        name="scatter",
    )(picks, near(returned))
    sent_back = across(grad_proj, "view", views)
    grads = pl.pallas_call(
        unproject_kernel,
        out_shape=tuple(jax.ShapeDtypeStruct(piece.shape, F32) for piece in pieces),
        in_specs=[vmem()] * 7,
        out_specs=tuple(vmem() for _ in pieces),
        name="unproject",
    )(*pieces, cameras, near(sent_back))
    g_means, g_scales, g_rot, g_logits, g_coefs = grads
    return (
        shown.transpose(1, 0, 2)[None],
        g_means.transpose(1, 0, 2),
        g_scales.transpose(1, 0, 2),
        g_rot,
        g_logits,
        g_coefs,
        grad_expo,
    )


def solution(mesh):
    return jax.shard_map(
        local,
        mesh=mesh,
        in_specs=(
            P(("view", "scene"), None, None),
            P(("view", "scene"), None, None),
            P(("view", "scene"), None, None),
            P(("view", "scene"), None, None),
            P(("view", "scene"), None, None),
            P(),
            P("view", None),
            P("view", "scene", None, None),
            P("view", "scene"),
            P("view", "scene", None, None),
            P("view", "scene", None),
        ),
        out_specs=(
            P("view", "scene", None, None),
            P(("view", "scene"), None, None),
            P(("view", "scene"), None, None),
            P(("view", "scene"), None, None),
            P(("view", "scene"), None, None),
            P(("view", "scene"), None, None),
            P("view", None),
        ),
        check_vma=False,
    )
```

```python
import jax
import jax.numpy as jnp
from jax import lax
from jax.experimental import pallas as pl
from jax.experimental.pallas import tpu as pltpu
from jax.sharding import PartitionSpec as P

PIX = 256
TILE_COLS = 32
G = 128
FEAT = 9
F32 = jnp.float32
BF16 = jnp.bfloat16
LOG2E = 1.4426950408889634

SH_ZERO = 0.28209479177387814
SH_ONE = 0.4886025119029199
SH_TWO = (
    1.0925484305920792,
    -1.0925484305920792,
    0.31539156525252005,
    -1.0925484305920792,
    0.5462742152960396,
)
SH_THREE = (
    -0.5900435899266435,
    2.890611442640554,
    -0.4570457994644658,
    0.3731763325901154,
    -0.4570457994644658,
    1.445305721320277,
    -0.5900435899266435,
)


def harmonics(dir_x, dir_y, dir_z):
    sq_x, sq_y, sq_z = (dir_x * dir_x, dir_y * dir_y, dir_z * dir_z)
    return [
        SH_ZERO * jnp.ones_like(dir_x),
        -SH_ONE * dir_y,
        SH_ONE * dir_z,
        -SH_ONE * dir_x,
        SH_TWO[0] * dir_x * dir_y,
        SH_TWO[1] * dir_y * dir_z,
        SH_TWO[2] * (2.0 * sq_z - sq_x - sq_y),
        SH_TWO[3] * dir_x * dir_z,
        SH_TWO[4] * (sq_x - sq_y),
        SH_THREE[0] * dir_y * (3.0 * sq_x - sq_y),
        SH_THREE[1] * dir_x * dir_y * dir_z,
        SH_THREE[2] * dir_y * (4.0 * sq_z - sq_x - sq_y),
        SH_THREE[3] * dir_z * (2.0 * sq_z - 3.0 * sq_x - 3.0 * sq_y),
        SH_THREE[4] * dir_x * (4.0 * sq_z - sq_x - sq_y),
        SH_THREE[5] * dir_z * (sq_x - sq_y),
        SH_THREE[6] * dir_x * (sq_x - 3.0 * sq_y),
    ]


def project(position, log_scales, quats, logit, coefs, cam):
    rotation = [[cam[3 * row + col] for col in range(3)] for row in range(3)]
    translation = cam[9:12]
    focal_x, focal_y, centre_x, centre_y = cam[12:16]
    view_pos = [
        rotation[row][0] * position[0]
        + rotation[row][1] * position[1]
        + rotation[row][2] * position[2]
        + translation[row]
        for row in range(3)
    ]
    inv_depth = 1.0 / view_pos[2]
    quat_w = quats[0] + 3.0
    quat_x, quat_y, quat_z = quats[1:4]
    quat_norm = jnp.sqrt(quat_w * quat_w + quat_x * quat_x + quat_y * quat_y + quat_z * quat_z)
    inv_norm = 1.0 / quat_norm
    quat_w, quat_x, quat_y, quat_z = (
        quat_w * inv_norm,
        quat_x * inv_norm,
        quat_y * inv_norm,
        quat_z * inv_norm,
    )
    spin = [
        [
            1.0 - 2.0 * (quat_y * quat_y + quat_z * quat_z),
            2.0 * (quat_x * quat_y - quat_w * quat_z),
            2.0 * (quat_x * quat_z + quat_w * quat_y),
        ],
        [
            2.0 * (quat_x * quat_y + quat_w * quat_z),
            1.0 - 2.0 * (quat_x * quat_x + quat_z * quat_z),
            2.0 * (quat_y * quat_z - quat_w * quat_x),
        ],
        [
            2.0 * (quat_x * quat_z - quat_w * quat_y),
            2.0 * (quat_y * quat_z + quat_w * quat_x),
            1.0 - 2.0 * (quat_x * quat_x + quat_y * quat_y),
        ],
    ]
    scales = [jnp.exp(row) for row in log_scales]
    world = [[spin[row][col] * scales[col] for col in range(3)] for row in range(3)]
    step_x = focal_x * inv_depth
    step_y = focal_y * inv_depth
    slide_x = step_x * view_pos[0] * inv_depth
    slide_y = step_y * view_pos[1] * inv_depth
    jac = [
        [step_x * rotation[0][col] - slide_x * rotation[2][col] for col in range(3)],
        [step_y * rotation[1][col] - slide_y * rotation[2][col] for col in range(3)],
    ]
    screen = [
        [
            jac[row][0] * world[0][col] + jac[row][1] * world[1][col] + jac[row][2] * world[2][col]
            for col in range(3)
        ]
        for row in range(2)
    ]
    sigma_xx = screen[0][0] * screen[0][0] + screen[0][1] * screen[0][1] + screen[0][2] * screen[0][2] + 0.3
    sigma_yy = screen[1][0] * screen[1][0] + screen[1][1] * screen[1][1] + screen[1][2] * screen[1][2] + 0.3
    sigma_xy = screen[0][0] * screen[1][0] + screen[0][1] * screen[1][1] + screen[0][2] * screen[1][2]
    inv_det = 1.0 / (sigma_xx * sigma_yy - sigma_xy * sigma_xy)
    screen_x = step_x * view_pos[0] + centre_x
    screen_y = step_y * view_pos[1] + centre_y
    opacity = 1.0 / (1.0 + jnp.exp(-logit))
    eye = [
        -(
            rotation[0][col] * translation[0]
            + rotation[1][col] * translation[1]
            + rotation[2][col] * translation[2]
        )
        for col in range(3)
    ]
    offs = [position[col] - eye[col] for col in range(3)]
    inv_dist = 1.0 / jnp.sqrt(offs[0] * offs[0] + offs[1] * offs[1] + offs[2] * offs[2])
    basis = harmonics(offs[0] * inv_dist, offs[1] * inv_dist, offs[2] * inv_dist)
    colours = []
    for channel in range(3):
        total = basis[0] * coefs[channel]
        for band in range(1, 16):
            total = total + basis[band] * coefs[3 * band + channel]
        colours.append(jnp.maximum(0.5 + total, 0.0))
    return [
        screen_x,
        screen_y,
        sigma_yy * inv_det,
        -sigma_xy * inv_det,
        sigma_xx * inv_det,
        opacity,
    ] + colours


KEPT = 64


def block_inputs(kept, block, views):
    def rows(first, count):
        start = block * KEPT + first
        return [jnp.broadcast_to(kept[start + r : start + r + 1, :], (views, G)) for r in range(count)]

    return (rows(0, 3), rows(3, 3), rows(6, 4), rows(10, 1)[0], rows(16, 48))


def camera_columns(cam_ref, views):
    cams = cam_ref[...]
    return [jnp.broadcast_to(cams[:, col : col + 1], (views, G)) for col in range(16)]


def project_kernel(
    means, log_scales, rotations, logits, coefs, cam_ref, picks, out_ref, kept, cam_kept, picks_kept
):
    views = cam_ref.shape[0]
    blocks = rotations.shape[0]
    cam_kept[...] = cam_ref[...]
    picks_kept[...] = picks[...]
    cam = camera_columns(cam_ref, views)
    for block in range(blocks):
        start = block * KEPT
        for r in range(3):
            kept[start + r : start + r + 1, :] = means[r, pl.ds(block, 1), :]
            kept[start + 3 + r : start + 4 + r, :] = log_scales[r, pl.ds(block, 1), :]
        kept[start + 6 : start + 10, :] = rotations[block]
        kept[start + 10 : start + 11, :] = logits[block]
        kept[start + 11 : start + 16, :] = jnp.zeros((5, G), F32)
        kept[start + 16 : start + KEPT, :] = coefs[block]
        for feat, value in enumerate(project(*block_inputs(kept, block, views), cam)):
            out_ref[pl.ds(block * FEAT + feat, views, stride=blocks * FEAT), :] = value


def unproject_kernel(kept, cam_ref, back_ref, o_means, o_scales, o_rot, o_logit, o_coef):
    views = cam_ref.shape[0]
    blocks = o_rot.shape[0]
    cam = camera_columns(cam_ref, views)

    def total(value):
        return jnp.sum(value, axis=0, keepdims=True)

    for block in range(blocks):
        pieces = block_inputs(kept, block, views)
        _, pull = jax.vjp(lambda *own: project(*own, cam), *pieces)
        seeds = [
            back_ref[pl.ds(block * FEAT + feat, views, stride=blocks * FEAT), :] for feat in range(FEAT)
        ]
        g_means, g_scales, g_rot, g_logit, g_coef = pull(seeds)
        for ref, rows in ((o_means, g_means), (o_scales, g_scales)):
            for row, value in enumerate(rows):
                ref[row, pl.ds(block, 1), :] = total(value)
        for ref, rows in ((o_rot, g_rot), (o_logit, [g_logit]), (o_coef, g_coef)):
            for row, value in enumerate(rows):
                ref[block, pl.ds(row, 1), :] = total(value)


def chosen(picks, cap, blocks):
    spots = lax.broadcasted_iota(jnp.int32, (blocks, picks.shape[1]), 0)
    return [jnp.where(spots == picks[c : c + 1, :], 1.0, 0.0) for c in range(cap)]


def gather_kernel(picks, src_ref, out_ref):
    cap, renderers = picks.shape
    blocks = src_ref.shape[0] // FEAT
    turned = [select.T.astype(BF16) for select in chosen(jnp.maximum(picks[...], 0), cap, blocks)]
    for feat in range(FEAT):
        pieces = [piece.astype(BF16) for piece in pieces3(src_ref[pl.ds(feat, blocks, stride=FEAT), :])]
        for c in range(cap):
            value = dot(turned[c], pieces[0]) + dot(turned[c], pieces[1]) + dot(turned[c], pieces[2])
            out_ref[pl.ds(c * FEAT + feat, renderers, stride=cap * FEAT), :] = value


def scatter_kernel(picks, src_ref, out_ref, expo_ref):
    cap, renderers = picks.shape
    stride = cap * FEAT + 1
    blocks = out_ref.shape[0] // FEAT
    selects = [select.astype(BF16) for select in chosen(picks[...], cap, blocks)]
    for feat in range(FEAT):
        total = jnp.zeros((blocks, G), F32)
        for c in range(cap):
            rows = src_ref[pl.ds(c * FEAT + feat, renderers, stride=stride), :]
            for piece in pieces3(rows):
                total = total + dot(selects[c], piece.astype(BF16))
        out_ref[pl.ds(feat, blocks, stride=FEAT), :] = total
    terms = src_ref[pl.ds(stride - 1, renderers, stride=stride), :]
    expo_ref[...] = jnp.sum(terms, axis=0, keepdims=True)[:, 0:12]


def split2(value):
    high = value.astype(BF16)
    low = (value - high.astype(F32)).astype(BF16)
    return high, low


def pieces3(value):
    high = value.astype(BF16).astype(F32)
    rest = value - high
    middle = rest.astype(BF16).astype(F32)
    return high, middle, rest - middle


def monomials(part, pixel):
    spot_x = (pixel % 16).astype(F32) - 7.5
    spot_y = (pixel // 16).astype(F32) - 7.5
    value = jnp.where(part == 0, 1.0, 0.0)
    value = jnp.where(part == 1, spot_x, value)
    value = jnp.where(part == 2, spot_y, value)
    value = jnp.where(part == 3, spot_x * spot_x, value)
    value = jnp.where(part == 4, spot_x * spot_y, value)
    return jnp.where(part == 5, spot_y * spot_y, value)


def dot(left, right):
    return jnp.dot(left, right, preferred_element_type=F32)


def dot_t(left, right):
    return lax.dot_general(left, right, (((1,), (1,)), ((), ())), preferred_element_type=F32)


ROWS = 32
PITCH = 9


def render_kernel(
    tile_ids,
    slots,
    expo,
    in_ref,
    goal_ref,
    shown_ref,
    grad_ref,
    raw,
    mat,
    mat_c,
    mat_b,
    left,
    mono,
    mono_t,
    al0,
    al1,
    wt0,
    wt1,
    gm0,
    gm1,
    hh0,
    hh1,
    wt_h,
    wt_l,
    ccol,
    gall,
    g_rhs,
    g_own,
    mom,
):
    kmax, tiles = slots.shape
    groups = tiles // 8
    picks = tiles * kmax
    cap = 2
    stride = cap * FEAT + 1
    scene = grad_ref.shape[0] // stride
    wide = 8 * ROWS
    rows16 = lax.broadcasted_iota(jnp.int32, (16, G), 0)
    lanes = lax.broadcasted_iota(jnp.int32, (1, G), 1)
    alphas, weights, slopes, moved = (al0, al1), (wt0, wt1), (gm0, gm1), (hh0, hh1)

    row = lax.broadcasted_iota(jnp.int32, (wide, PIX), 0) // 8
    part = jnp.where(row < 18, row % 6, 6)
    mono[...] = monomials(part, lax.broadcasted_iota(jnp.int32, (wide, PIX), 1)).astype(BF16)
    part = lax.broadcasted_iota(jnp.int32, (16, PIX), 0)
    mono_t[...] = monomials(part, lax.broadcasted_iota(jnp.int32, (16, PIX), 1)).astype(BF16)

    def place(group, k, t):
        return (group * kmax + k) * 8 + t

    for group in range(groups):
        for t in range(8):
            tile = group * 8 + t
            tile_id = tile_ids[tile]
            mid_x = ((tile_id % TILE_COLS) * 16 + 8).astype(F32)
            mid_y = ((tile_id // TILE_COLS) * 16 + 8).astype(F32)
            shift = jnp.where(rows16 == 0, mid_x, jnp.where(rows16 == 1, mid_y, 0.0))
            for k in range(kmax):
                slot = slots[k, tile]
                base = jnp.maximum(slot, 0) * FEAT
                spot = place(group, k, t) * 16
                raw[spot : spot + FEAT, :] = in_ref[pl.ds(base, FEAT), :] - shift[0:FEAT]
                raw[spot + FEAT : spot + FEAT + 1, :] = jnp.full((1, G), jnp.where(slot < 0, -4000.0, 0.0))

    def feature(index):
        return raw[pl.ds(index, picks, stride=16), :]

    off_x, off_y, con_a, con_b, con_c, opac = [feature(i) for i in range(6)]
    poly_a = con_a * (-0.5 * LOG2E)
    poly_b = con_b * (-LOG2E)
    poly_c = con_c * (-0.5 * LOG2E)
    lead = poly_a * off_x + poly_b * off_y
    tail = poly_c * off_y
    coefs = [
        off_x * lead + off_y * tail + jnp.log(opac) * LOG2E + feature(FEAT),
        -(lead + poly_a * off_x),
        -(2.0 * tail + poly_b * off_x),
        poly_a,
        poly_b,
        poly_c,
    ]
    blank = jnp.zeros((8, G), F32)
    rows_of = [blank] * ROWS
    for index in range(6):
        for piece, value in enumerate(pieces3(coefs[index])):
            rows_of[6 * piece + index] = value
    mat_c[...] = jnp.zeros(mat_c.shape, F32)
    for channel in range(3):
        high, middle, _ = pieces3(feature(6 + channel))
        rows_of[18 + channel] = high
        rows_of[21 + channel] = middle
        rows_of[24 + channel] = high
        mat_c[pl.ds(channel, picks, stride=16), :] = high
        mat_c[pl.ds(3 + channel, picks, stride=16), :] = middle
    for chunk in range(groups * kmax):
        for index, value in enumerate(rows_of):
            start = chunk * wide + index * 8
            mat[start : start + 8, :] = value if index >= 27 else value[chunk * 8 : chunk * 8 + 8]
    mat_b[...] = mat_c[...].astype(BF16)

    lane_tile = lax.broadcasted_iota(jnp.int32, (1, wide), 1) % 8
    masks = [jnp.where(lane_tile == t, 1.0, 0.0).astype(BF16) for t in range(8)]

    for chunk in range(groups * kmax):
        sides = [mat[chunk * wide + half * G : chunk * wide + (half + 1) * G, :].T for half in range(2)]
        turned = jnp.concatenate(sides, axis=1).astype(BF16)
        left[chunk * G : (chunk + 1) * G, :] = turned
        for t in range(8):
            alpha = jnp.exp2(dot(turned * masks[t], mono[...]))
            for half in range(2):
                alphas[half][pl.ds(chunk * G * PITCH + t, G, stride=PITCH), :] = alpha[:, half * G : (half + 1) * G]

    count = kmax * G

    batch = 8

    def forward(step, keeps):
        keeps = list(keeps)
        base = step * (batch * PITCH)
        for inner in range(batch):
            for group in range(groups):
                rows = pl.ds(base + (group * count + inner) * PITCH, 8)
                for half in range(2):
                    at = group * 2 + half
                    alpha = alphas[half][rows, :]
                    weights[half][rows, :] = keeps[at] * alpha
                    keeps[at] = keeps[at] * (1.0 - alpha)
        return tuple(keeps)

    ones = jnp.ones((8, G), F32)
    lax.fori_loop(0, count // batch, forward, (ones,) * (2 * groups))

    for group in range(groups):
        for t in range(8):
            total = jnp.zeros((16, PIX), F32)
            for k in range(kmax):
                spot = place(group, k, t)
                rows = pl.ds((group * kmax + k) * G * PITCH + t, G, stride=PITCH)
                weight = jnp.concatenate([weights[0][rows, :], weights[1][rows, :]], axis=1)
                w_high, w_low = split2(weight)
                wt_h[spot * G : (spot + 1) * G, :] = w_high
                wt_l[spot * G : (spot + 1) * G, :] = w_low
                own = mat_b[spot * 16 : (spot + 1) * 16, :]
                total = total + dot(own, wt_h[spot * G : (spot + 1) * G, :])
                total = total + dot(own, wt_l[spot * G : (spot + 1) * G, :])
            for channel in range(3):
                row = channel * tiles + group * 8 + t
                ccol[row : row + 1, :] = total[channel : channel + 1, :] + total[3 + channel : 4 + channel, :]

    colour = [ccol[c * tiles : (c + 1) * tiles, :] for c in range(3)]
    miss = []
    for i in range(3):
        value = colour[i] + expo[0, 9 + i]
        for j in range(3):
            value = value + expo[0, 3 * i + j] * colour[j]
        shown_ref[i] = value
        miss.append(value - goal_ref[i])
    slope = []
    for j in range(3):
        value = miss[j]
        for i in range(3):
            value = value + expo[0, 3 * i + j] * miss[i]
        slope.append(value)
    terms = [miss[i] * colour[j] for i in range(3) for j in range(3)] + miss
    expo_row = jnp.zeros((1, G), F32)
    for index, value in enumerate(terms):
        folded = jnp.sum(value[:, 0:G] + value[:, G : 2 * G], axis=0, keepdims=True)
        expo_row = jnp.where(lanes == index, jnp.sum(folded, axis=1, keepdims=True), expo_row)

    highs = [value.astype(BF16).astype(F32) for value in slope]
    lows = [value - high for value, high in zip(slope, highs)]
    for group in range(groups):
        span = slice(group * 8, group * 8 + 8)
        nine = [value[span] for value in highs + highs + lows]
        stack = [jnp.zeros((18 * 8, PIX), F32)] + nine + [jnp.zeros(((ROWS - 27) * 8, PIX), F32)]
        g_rhs[group * wide : (group + 1) * wide, :] = jnp.concatenate(stack, axis=0).astype(BF16)
    gall[...] = jnp.zeros(gall.shape, F32)
    for half in range(2):
        side = slice(half * G, (half + 1) * G)
        for channel in range(3):
            gall[pl.ds(channel, tiles, stride=16), :] = highs[channel][:, side]
            gall[pl.ds(3 + channel, tiles, stride=16), :] = lows[channel][:, side]
        g_own[:, side] = gall[...].astype(BF16)
    for chunk in range(groups * kmax):
        turned = left[chunk * G : (chunk + 1) * G, :]
        group = chunk // kmax
        right = g_rhs[group * wide : (group + 1) * wide, :]
        for t in range(8):
            value = dot(turned * masks[t], right)
            for half in range(2):
                slopes[half][pl.ds(chunk * G * PITCH + t, G, stride=PITCH), :] = value[:, half * G : (half + 1) * G]

    def backward(step, behind):
        behind = list(behind)
        base = (count - batch - step * batch) * PITCH
        for inner in range(batch - 1, -1, -1):
            for group in range(groups):
                rows = pl.ds(base + (group * count + inner) * PITCH, 8)
                for half in range(2):
                    at = group * 2 + half
                    alpha = alphas[half][rows, :]
                    value = slopes[half][rows, :]
                    moved[half][rows, :] = weights[half][rows, :] * (value - behind[at])
                    behind[at] = behind[at] * (1.0 - alpha) + alpha * value
        return tuple(behind)

    zeros = jnp.zeros((8, G), F32)
    lax.fori_loop(0, count // batch, backward, (zeros,) * (2 * groups))

    for group in range(groups):
        for k in range(kmax):
            for t in range(8):
                spot = place(group, k, t)
                rows = pl.ds((group * kmax + k) * G * PITCH + t, G, stride=PITCH)
                value = jnp.concatenate([moved[0][rows, :].T, moved[1][rows, :].T], axis=0)
                v_high, v_low = split2(value)
                table = mono_t[...]
                sums = dot(table, v_high) + dot(table, v_low)
                mom[spot * PITCH : spot * PITCH + 8, :] = sums[0:8]
                own = g_own[(group * 8 + t) * 16 : (group * 8 + t + 1) * 16, :]
                w_high = wt_h[spot * G : (spot + 1) * G, :]
                w_low = wt_l[spot * G : (spot + 1) * G, :]
                mat_c[spot * 16 : (spot + 1) * 16, :] = dot_t(own, w_high) + dot_t(own, w_low)

    sum_0, sum_x, sum_y, sum_xx, sum_xy, sum_yy = [mom[pl.ds(i, picks, stride=PITCH), :] for i in range(6)]
    off_x, off_y, con_a, con_b, con_c, opac = [feature(i) for i in range(6)]
    cen_x = sum_x - off_x * sum_0
    cen_y = sum_y - off_y * sum_0
    cen_xx = sum_xx - off_x * (sum_x + cen_x)
    cen_yy = sum_yy - off_y * (sum_y + cen_y)
    cen_xy = sum_xy - off_x * sum_y - off_y * cen_x
    outs = [
        con_a * cen_x + con_b * cen_y,
        con_b * cen_x + con_c * cen_y,
        -0.5 * cen_xx,
        -cen_xy,
        -0.5 * cen_yy,
        sum_0 / opac,
    ]
    for channel in range(3):
        outs.append(
            mat_c[pl.ds(channel, picks, stride=16), :] + mat_c[pl.ds(3 + channel, picks, stride=16), :]
        )
    for index, value in enumerate(outs):
        raw[pl.ds(index, picks, stride=16), :] = value

    grad_ref[...] = jnp.zeros(grad_ref.shape, F32)
    for group in range(groups):
        for k in range(kmax):
            for t in range(8):
                slot = jnp.maximum(slots[k, group * 8 + t], 0)
                where = pl.ds((slot // cap) * stride + (slot % cap) * FEAT, FEAT)
                spot = place(group, k, t) * 16
                grad_ref[where, :] = grad_ref[where, :] + raw[spot : spot + FEAT, :]
    grad_ref[pl.ds(stride - 1, scene, stride=stride), :] = jnp.broadcast_to(expo_row, (scene, G))


def vmem():
    return pl.BlockSpec(memory_space=pltpu.VMEM)


def smem():
    return pl.BlockSpec(memory_space=pltpu.SMEM)


def across(rows, axis, parts):
    shaped = rows.reshape(parts, rows.shape[0] // parts, 1, G)
    moved = lax.all_to_all(shaped, axis, split_axis=0, concat_axis=0, tiled=True)
    return moved.reshape(rows.shape)


def near(rows):
    return pltpu.with_memory_space_constraint(rows, pltpu.VMEM)


def render(tile_ids, slots, expo, incoming, goal, interpret=False):
    kmax, tiles = slots.shape
    picks = tiles * kmax
    groups = tiles // 8
    scene = incoming.shape[0] // (2 * FEAT)
    big = pltpu.VMEM((picks // 8 * G * PITCH, G), F32)
    return pl.pallas_call(
        render_kernel,
        out_shape=(
            jax.ShapeDtypeStruct((3, tiles, PIX), F32),
            pltpu.VMEM((scene * (2 * FEAT + 1), G), F32),
        ),
        in_specs=[smem(), smem(), smem(), vmem(), vmem()],
        out_specs=(vmem(), vmem()),
        scratch_shapes=[
            pltpu.VMEM((picks * 16, G), F32),
            pltpu.VMEM((picks * ROWS, G), F32),
            pltpu.VMEM((picks * 16, G), F32),
            pltpu.VMEM((picks * 16, G), BF16),
            pltpu.VMEM((groups * kmax * G, 8 * ROWS), BF16),
            pltpu.VMEM((8 * ROWS, PIX), BF16),
            pltpu.VMEM((16, PIX), BF16),
            big,
            big,
            big,
            big,
            big,
            big,
            big,
            big,
            pltpu.VMEM((picks * G, PIX), BF16),
            pltpu.VMEM((picks * G, PIX), BF16),
            pltpu.VMEM((3 * tiles, PIX), F32),
            pltpu.VMEM((tiles * 16, G), F32),
            pltpu.VMEM((tiles * ROWS, PIX), BF16),
            pltpu.VMEM((tiles * 16, PIX), BF16),
            pltpu.VMEM((picks * PITCH, G), F32),
        ],
        compiler_params=pltpu.CompilerParams(vmem_limit_bytes=56 * 1024 * 1024),
        name="render",
        interpret=interpret,
    )(tile_ids, slots, expo, incoming, goal)


def local(
    means,
    log_scales,
    rotations,
    opacity_logits,
    colour_coefs,
    cameras,
    exposure,
    target,
    tile_ids,
    send_list,
    pair_slots,
):
    views = lax.axis_size("view")
    scene = lax.axis_size("scene")
    blocks = means.shape[0]
    cap = send_list.shape[3]
    pieces = (
        means.transpose(1, 0, 2),
        log_scales.transpose(1, 0, 2),
        rotations,
        opacity_logits,
        colour_coefs,
    )
    picks = send_list[0, 0].T
    own_count = views * blocks * FEAT
    own_proj, kept, cams, picks = pl.pallas_call(
        project_kernel,
        out_shape=(
            pltpu.VMEM((own_count, G), F32),
            pltpu.VMEM((blocks * KEPT, G), F32),
            pltpu.VMEM(cameras.shape, F32),
            pltpu.VMEM(picks.shape, picks.dtype),
        ),
        in_specs=[vmem()] * 7,
        out_specs=(vmem(),) * 4,
        name="project",
    )(*pieces, cameras, picks)
    projected = across(own_proj, "view", views)
    outgoing = pl.pallas_call(
        gather_kernel,
        out_shape=pltpu.VMEM((scene * cap * FEAT, G), F32),
        in_specs=[vmem(), vmem()],
        out_specs=vmem(),
        name="gather",
    )(near(picks), near(projected))
    incoming = across(outgoing, "scene", scene)
    shown, grad_rows = render(
        tile_ids[0], pair_slots[0].T, exposure, near(incoming), near(target[0].transpose(1, 0, 2))
    )
    returned = across(grad_rows, "scene", scene)
    grad_proj, grad_expo = pl.pallas_call(
        scatter_kernel,
        out_shape=(pltpu.VMEM((own_count, G), F32), jax.ShapeDtypeStruct((1, 12), F32)),
        in_specs=[vmem(), vmem()],
        out_specs=(vmem(), vmem()),
        name="scatter",
    )(near(picks), near(returned))
    sent_back = across(grad_proj, "view", views)
    grads = pl.pallas_call(
        unproject_kernel,
        out_shape=tuple(jax.ShapeDtypeStruct(piece.shape, F32) for piece in pieces),
        in_specs=[vmem()] * 3,
        out_specs=tuple(vmem() for _ in pieces),
        name="unproject",
    )(near(kept), near(cams), near(sent_back))
    g_means, g_scales, g_rot, g_logits, g_coefs = grads
    return (
        shown.transpose(1, 0, 2)[None],
        g_means.transpose(1, 0, 2),
        g_scales.transpose(1, 0, 2),
        g_rot,
        g_logits,
        g_coefs,
        grad_expo,
    )


def solution(mesh):
    return jax.shard_map(
        local,
        mesh=mesh,
        in_specs=(
            P(("view", "scene"), None, None),
            P(("view", "scene"), None, None),
            P(("view", "scene"), None, None),
            P(("view", "scene"), None, None),
            P(("view", "scene"), None, None),
            P(),
            P("view", None),
            P("view", "scene", None, None),
            P("view", "scene"),
            P("view", "scene", None, None),
            P("view", "scene", None),
        ),
        out_specs=(
            P("view", "scene", None, None),
            P(("view", "scene"), None, None),
            P(("view", "scene"), None, None),
            P(("view", "scene"), None, None),
            P(("view", "scene"), None, None),
            P(("view", "scene"), None, None),
            P("view", None),
        ),
        check_vma=False,
    )
```

```python
import jax
import jax.numpy as jnp
from jax import lax
from jax.experimental import pallas as pl
from jax.experimental.pallas import tpu as pltpu
from jax.sharding import PartitionSpec as P

PIX = 256
TILE_COLS = 32
G = 128
FEAT = 9
F32 = jnp.float32
BF16 = jnp.bfloat16
LOG2E = 1.4426950408889634

SH_ZERO = 0.28209479177387814
SH_ONE = 0.4886025119029199
SH_TWO = (
    1.0925484305920792,
    -1.0925484305920792,
    0.31539156525252005,
    -1.0925484305920792,
    0.5462742152960396,
)
SH_THREE = (
    -0.5900435899266435,
    2.890611442640554,
    -0.4570457994644658,
    0.3731763325901154,
    -0.4570457994644658,
    1.445305721320277,
    -0.5900435899266435,
)


def harmonics(dir_x, dir_y, dir_z):
    sq_x, sq_y, sq_z = (dir_x * dir_x, dir_y * dir_y, dir_z * dir_z)
    return [
        SH_ZERO * jnp.ones_like(dir_x),
        -SH_ONE * dir_y,
        SH_ONE * dir_z,
        -SH_ONE * dir_x,
        SH_TWO[0] * dir_x * dir_y,
        SH_TWO[1] * dir_y * dir_z,
        SH_TWO[2] * (2.0 * sq_z - sq_x - sq_y),
        SH_TWO[3] * dir_x * dir_z,
        SH_TWO[4] * (sq_x - sq_y),
        SH_THREE[0] * dir_y * (3.0 * sq_x - sq_y),
        SH_THREE[1] * dir_x * dir_y * dir_z,
        SH_THREE[2] * dir_y * (4.0 * sq_z - sq_x - sq_y),
        SH_THREE[3] * dir_z * (2.0 * sq_z - 3.0 * sq_x - 3.0 * sq_y),
        SH_THREE[4] * dir_x * (4.0 * sq_z - sq_x - sq_y),
        SH_THREE[5] * dir_z * (sq_x - sq_y),
        SH_THREE[6] * dir_x * (sq_x - 3.0 * sq_y),
    ]


def project(position, log_scales, quats, logit, coefs, cam):
    rotation = [[cam[3 * row + col] for col in range(3)] for row in range(3)]
    translation = cam[9:12]
    focal_x, focal_y, centre_x, centre_y = cam[12:16]
    view_pos = [
        rotation[row][0] * position[0]
        + rotation[row][1] * position[1]
        + rotation[row][2] * position[2]
        + translation[row]
        for row in range(3)
    ]
    inv_depth = 1.0 / view_pos[2]
    quat_w = quats[0] + 3.0
    quat_x, quat_y, quat_z = quats[1:4]
    quat_norm = jnp.sqrt(quat_w * quat_w + quat_x * quat_x + quat_y * quat_y + quat_z * quat_z)
    inv_norm = 1.0 / quat_norm
    quat_w, quat_x, quat_y, quat_z = (
        quat_w * inv_norm,
        quat_x * inv_norm,
        quat_y * inv_norm,
        quat_z * inv_norm,
    )
    spin = [
        [
            1.0 - 2.0 * (quat_y * quat_y + quat_z * quat_z),
            2.0 * (quat_x * quat_y - quat_w * quat_z),
            2.0 * (quat_x * quat_z + quat_w * quat_y),
        ],
        [
            2.0 * (quat_x * quat_y + quat_w * quat_z),
            1.0 - 2.0 * (quat_x * quat_x + quat_z * quat_z),
            2.0 * (quat_y * quat_z - quat_w * quat_x),
        ],
        [
            2.0 * (quat_x * quat_z - quat_w * quat_y),
            2.0 * (quat_y * quat_z + quat_w * quat_x),
            1.0 - 2.0 * (quat_x * quat_x + quat_y * quat_y),
        ],
    ]
    scales = [jnp.exp(row) for row in log_scales]
    world = [[spin[row][col] * scales[col] for col in range(3)] for row in range(3)]
    step_x = focal_x * inv_depth
    step_y = focal_y * inv_depth
    slide_x = step_x * view_pos[0] * inv_depth
    slide_y = step_y * view_pos[1] * inv_depth
    jac = [
        [step_x * rotation[0][col] - slide_x * rotation[2][col] for col in range(3)],
        [step_y * rotation[1][col] - slide_y * rotation[2][col] for col in range(3)],
    ]
    screen = [
        [
            jac[row][0] * world[0][col] + jac[row][1] * world[1][col] + jac[row][2] * world[2][col]
            for col in range(3)
        ]
        for row in range(2)
    ]
    sigma_xx = screen[0][0] * screen[0][0] + screen[0][1] * screen[0][1] + screen[0][2] * screen[0][2] + 0.3
    sigma_yy = screen[1][0] * screen[1][0] + screen[1][1] * screen[1][1] + screen[1][2] * screen[1][2] + 0.3
    sigma_xy = screen[0][0] * screen[1][0] + screen[0][1] * screen[1][1] + screen[0][2] * screen[1][2]
    inv_det = 1.0 / (sigma_xx * sigma_yy - sigma_xy * sigma_xy)
    screen_x = step_x * view_pos[0] + centre_x
    screen_y = step_y * view_pos[1] + centre_y
    opacity = 1.0 / (1.0 + jnp.exp(-logit))
    eye = [
        -(
            rotation[0][col] * translation[0]
            + rotation[1][col] * translation[1]
            + rotation[2][col] * translation[2]
        )
        for col in range(3)
    ]
    offs = [position[col] - eye[col] for col in range(3)]
    inv_dist = 1.0 / jnp.sqrt(offs[0] * offs[0] + offs[1] * offs[1] + offs[2] * offs[2])
    basis = harmonics(offs[0] * inv_dist, offs[1] * inv_dist, offs[2] * inv_dist)
    colours = []
    for channel in range(3):
        total = basis[0] * coefs[channel]
        for band in range(1, 16):
            total = total + basis[band] * coefs[3 * band + channel]
        colours.append(jnp.maximum(0.5 + total, 0.0))
    return [
        screen_x,
        screen_y,
        sigma_yy * inv_det,
        -sigma_xy * inv_det,
        sigma_xx * inv_det,
        opacity,
    ] + colours


KEPT = 64


def block_inputs(kept, block, views):
    def rows(first, count):
        start = block * KEPT + first
        return [jnp.broadcast_to(kept[start + r : start + r + 1, :], (views, G)) for r in range(count)]

    return (rows(0, 3), rows(3, 3), rows(6, 4), rows(10, 1)[0], rows(16, 48))


def camera_columns(cam_ref, views):
    cams = cam_ref[...]
    return [jnp.broadcast_to(cams[:, col : col + 1], (views, G)) for col in range(16)]


def project_kernel(
    means, log_scales, rotations, logits, coefs, cam_ref, picks, out_ref, kept, cam_kept, picks_kept
):
    views = cam_ref.shape[0]
    blocks = rotations.shape[0]
    cam_kept[...] = cam_ref[...]
    picks_kept[...] = picks[...]
    cam = camera_columns(cam_ref, views)
    for block in range(blocks):
        start = block * KEPT
        for r in range(3):
            kept[start + r : start + r + 1, :] = means[r, pl.ds(block, 1), :]
            kept[start + 3 + r : start + 4 + r, :] = log_scales[r, pl.ds(block, 1), :]
        kept[start + 6 : start + 10, :] = rotations[block]
        kept[start + 10 : start + 11, :] = logits[block]
        kept[start + 11 : start + 16, :] = jnp.zeros((5, G), F32)
        kept[start + 16 : start + KEPT, :] = coefs[block]
        for feat, value in enumerate(project(*block_inputs(kept, block, views), cam)):
            out_ref[pl.ds(block * FEAT + feat, views, stride=blocks * FEAT), :] = value


def unproject_kernel(kept, cam_ref, back_ref, o_means, o_scales, o_rot, o_logit, o_coef):
    views = cam_ref.shape[0]
    blocks = o_rot.shape[0]
    cam = camera_columns(cam_ref, views)

    def total(value):
        return jnp.sum(value, axis=0, keepdims=True)

    for block in range(blocks):
        pieces = block_inputs(kept, block, views)
        _, pull = jax.vjp(lambda *own: project(*own, cam), *pieces)
        seeds = [
            back_ref[pl.ds(block * FEAT + feat, views, stride=blocks * FEAT), :] for feat in range(FEAT)
        ]
        g_means, g_scales, g_rot, g_logit, g_coef = pull(seeds)
        for ref, rows in ((o_means, g_means), (o_scales, g_scales)):
            for row, value in enumerate(rows):
                ref[row, pl.ds(block, 1), :] = total(value)
        for ref, rows in ((o_rot, g_rot), (o_logit, [g_logit]), (o_coef, g_coef)):
            for row, value in enumerate(rows):
                ref[block, pl.ds(row, 1), :] = total(value)


def chosen(picks, cap, blocks):
    spots = lax.broadcasted_iota(jnp.int32, (blocks, picks.shape[1]), 0)
    return [jnp.where(spots == picks[c : c + 1, :], 1.0, 0.0) for c in range(cap)]


def gather_kernel(picks, src_ref, out_ref):
    cap, renderers = picks.shape
    blocks = src_ref.shape[0] // FEAT
    turned = [select.T.astype(BF16) for select in chosen(jnp.maximum(picks[...], 0), cap, blocks)]
    for feat in range(FEAT):
        pieces = [piece.astype(BF16) for piece in pieces3(src_ref[pl.ds(feat, blocks, stride=FEAT), :])]
        for c in range(cap):
            value = dot(turned[c], pieces[0]) + dot(turned[c], pieces[1]) + dot(turned[c], pieces[2])
            out_ref[pl.ds(c * FEAT + feat, renderers, stride=cap * FEAT), :] = value


def scatter_kernel(picks, src_ref, out_ref, expo_ref):
    cap, renderers = picks.shape
    stride = cap * FEAT + 1
    blocks = out_ref.shape[0] // FEAT
    selects = [select.astype(BF16) for select in chosen(picks[...], cap, blocks)]
    for feat in range(FEAT):
        total = jnp.zeros((blocks, G), F32)
        for c in range(cap):
            rows = src_ref[pl.ds(c * FEAT + feat, renderers, stride=stride), :]
            for piece in pieces3(rows):
                total = total + dot(selects[c], piece.astype(BF16))
        out_ref[pl.ds(feat, blocks, stride=FEAT), :] = total
    terms = src_ref[pl.ds(stride - 1, renderers, stride=stride), :]
    expo_ref[...] = jnp.sum(terms, axis=0, keepdims=True)[:, 0:12]


def split2(value):
    high = value.astype(BF16)
    low = (value - high.astype(F32)).astype(BF16)
    return high, low


def pieces3(value):
    high = value.astype(BF16).astype(F32)
    rest = value - high
    middle = rest.astype(BF16).astype(F32)
    return high, middle, rest - middle


def monomials(part, pixel):
    spot_x = (pixel % 16).astype(F32) - 7.5
    spot_y = (pixel // 16).astype(F32) - 7.5
    value = jnp.where(part == 0, 1.0, 0.0)
    value = jnp.where(part == 1, spot_x, value)
    value = jnp.where(part == 2, spot_y, value)
    value = jnp.where(part == 3, spot_x * spot_x, value)
    value = jnp.where(part == 4, spot_x * spot_y, value)
    return jnp.where(part == 5, spot_y * spot_y, value)


def dot(left, right):
    return jnp.dot(left, right, preferred_element_type=F32)


def dot_t(left, right):
    return lax.dot_general(left, right, (((1,), (1,)), ((), ())), preferred_element_type=F32)


ROWS = 32
PITCH = 9


def render_kernel(
    tile_ids,
    slots,
    expo,
    in_ref,
    goal_ref,
    shown_ref,
    grad_ref,
    raw,
    mat,
    mat_c,
    mat_b,
    left,
    mono,
    mono_t,
    al0,
    al1,
    wt0,
    wt1,
    gm0,
    gm1,
    hh0,
    hh1,
    wt_h,
    wt_l,
    ccol,
    gall,
    g_rhs,
    g_own,
    mom,
):
    kmax, tiles = slots.shape
    groups = tiles // 8
    picks = tiles * kmax
    cap = 2
    stride = cap * FEAT + 1
    scene = grad_ref.shape[0] // stride
    wide = 8 * ROWS
    rows16 = lax.broadcasted_iota(jnp.int32, (16, G), 0)
    lanes = lax.broadcasted_iota(jnp.int32, (1, G), 1)
    alphas, weights, slopes, moved = (al0, al1), (wt0, wt1), (gm0, gm1), (hh0, hh1)

    row = lax.broadcasted_iota(jnp.int32, (wide, PIX), 0) // 8
    part = jnp.where(row < 18, row % 6, 6)
    mono[...] = monomials(part, lax.broadcasted_iota(jnp.int32, (wide, PIX), 1)).astype(BF16)
    part = lax.broadcasted_iota(jnp.int32, (16, PIX), 0)
    mono_t[...] = monomials(part, lax.broadcasted_iota(jnp.int32, (16, PIX), 1)).astype(BF16)

    def place(group, k, t):
        return (group * kmax + k) * 8 + t

    for group in range(groups):
        for t in range(8):
            tile = group * 8 + t
            tile_id = tile_ids[tile]
            mid_x = ((tile_id % TILE_COLS) * 16 + 8).astype(F32)
            mid_y = ((tile_id // TILE_COLS) * 16 + 8).astype(F32)
            shift = jnp.where(rows16 == 0, mid_x, jnp.where(rows16 == 1, mid_y, 0.0))
            for k in range(kmax):
                slot = slots[k, tile]
                base = jnp.maximum(slot, 0) * FEAT
                spot = place(group, k, t) * 16
                raw[spot : spot + FEAT, :] = in_ref[pl.ds(base, FEAT), :] - shift[0:FEAT]
                raw[spot + FEAT : spot + FEAT + 1, :] = jnp.full((1, G), jnp.where(slot < 0, -4000.0, 0.0))

    def feature(index):
        return raw[pl.ds(index, picks, stride=16), :]

    off_x, off_y, con_a, con_b, con_c, opac = [feature(i) for i in range(6)]
    poly_a = con_a * (-0.5 * LOG2E)
    poly_b = con_b * (-LOG2E)
    poly_c = con_c * (-0.5 * LOG2E)
    lead = poly_a * off_x + poly_b * off_y
    tail = poly_c * off_y
    coefs = [
        off_x * lead + off_y * tail + jnp.log(opac) * LOG2E + feature(FEAT),
        -(lead + poly_a * off_x),
        -(2.0 * tail + poly_b * off_x),
        poly_a,
        poly_b,
        poly_c,
    ]
    blank = jnp.zeros((8, G), F32)
    rows_of = [blank] * ROWS
    for index in range(6):
        for piece, value in enumerate(pieces3(coefs[index])):
            rows_of[6 * piece + index] = value
    mat_c[...] = jnp.zeros(mat_c.shape, F32)
    for channel in range(3):
        high, middle, _ = pieces3(feature(6 + channel))
        rows_of[18 + channel] = high
        rows_of[21 + channel] = middle
        rows_of[24 + channel] = high
        mat_c[pl.ds(channel, picks, stride=16), :] = high
        mat_c[pl.ds(3 + channel, picks, stride=16), :] = middle
    for chunk in range(groups * kmax):
        for index, value in enumerate(rows_of):
            start = chunk * wide + index * 8
            mat[start : start + 8, :] = value if index >= 27 else value[chunk * 8 : chunk * 8 + 8]
    mat_b[...] = mat_c[...].astype(BF16)

    lane_tile = lax.broadcasted_iota(jnp.int32, (1, wide), 1) % 8
    masks = [jnp.where(lane_tile == t, 1.0, 0.0).astype(BF16) for t in range(8)]

    for chunk in range(groups * kmax):
        sides = [mat[chunk * wide + half * G : chunk * wide + (half + 1) * G, :].T for half in range(2)]
        turned = jnp.concatenate(sides, axis=1).astype(BF16)
        left[chunk * G : (chunk + 1) * G, :] = turned
        for t in range(8):
            alpha = jnp.exp2(dot(turned * masks[t], mono[...]))
            for half in range(2):
                alphas[half][pl.ds(chunk * G * PITCH + t, G, stride=PITCH), :] = alpha[:, half * G : (half + 1) * G]

    count = kmax * G

    batch = 16

    def forward(step, keeps):
        keeps = list(keeps)
        base = step * (batch * PITCH)
        for inner in range(batch):
            for group in range(groups):
                rows = pl.ds(base + (group * count + inner) * PITCH, 8)
                for half in range(2):
                    at = group * 2 + half
                    alpha = alphas[half][rows, :]
                    weights[half][rows, :] = keeps[at] * alpha
                    keeps[at] = keeps[at] * (1.0 - alpha)
        return tuple(keeps)

    ones = jnp.ones((8, G), F32)
    lax.fori_loop(0, count // batch, forward, (ones,) * (2 * groups))

    for group in range(groups):
        for t in range(8):
            total = jnp.zeros((16, PIX), F32)
            for k in range(kmax):
                spot = place(group, k, t)
                rows = pl.ds((group * kmax + k) * G * PITCH + t, G, stride=PITCH)
                weight = jnp.concatenate([weights[0][rows, :], weights[1][rows, :]], axis=1)
                w_high, w_low = split2(weight)
                kept = ((group * 8 + t) * kmax + k) * G
                wt_h[kept : kept + G, :] = w_high
                wt_l[kept : kept + G, :] = w_low
                own = mat_b[spot * 16 : (spot + 1) * 16, :]
                total = total + dot(own, wt_h[kept : kept + G, :])
                total = total + dot(own, wt_l[kept : kept + G, :])
            for channel in range(3):
                row = channel * tiles + group * 8 + t
                ccol[row : row + 1, :] = total[channel : channel + 1, :] + total[3 + channel : 4 + channel, :]

    colour = [ccol[c * tiles : (c + 1) * tiles, :] for c in range(3)]
    miss = []
    for i in range(3):
        value = colour[i] + expo[0, 9 + i]
        for j in range(3):
            value = value + expo[0, 3 * i + j] * colour[j]
        shown_ref[i] = value
        miss.append(value - goal_ref[i])
    slope = []
    for j in range(3):
        value = miss[j]
        for i in range(3):
            value = value + expo[0, 3 * i + j] * miss[i]
        slope.append(value)
    terms = [miss[i] * colour[j] for i in range(3) for j in range(3)] + miss
    expo_row = jnp.zeros((1, G), F32)
    for index, value in enumerate(terms):
        folded = jnp.sum(value[:, 0:G] + value[:, G : 2 * G], axis=0, keepdims=True)
        expo_row = jnp.where(lanes == index, jnp.sum(folded, axis=1, keepdims=True), expo_row)

    highs = [value.astype(BF16).astype(F32) for value in slope]
    lows = [value - high for value, high in zip(slope, highs)]
    for group in range(groups):
        span = slice(group * 8, group * 8 + 8)
        nine = [value[span] for value in highs + highs + lows]
        stack = [jnp.zeros((18 * 8, PIX), F32)] + nine + [jnp.zeros(((ROWS - 27) * 8, PIX), F32)]
        g_rhs[group * wide : (group + 1) * wide, :] = jnp.concatenate(stack, axis=0).astype(BF16)
    gall[...] = jnp.zeros(gall.shape, F32)
    for half in range(2):
        side = slice(half * G, (half + 1) * G)
        for channel in range(3):
            gall[pl.ds(channel, tiles, stride=16), :] = highs[channel][:, side]
            gall[pl.ds(3 + channel, tiles, stride=16), :] = lows[channel][:, side]
        g_own[:, side] = gall[...].astype(BF16)
    for chunk in range(groups * kmax):
        turned = left[chunk * G : (chunk + 1) * G, :]
        group = chunk // kmax
        right = g_rhs[group * wide : (group + 1) * wide, :]
        for t in range(8):
            value = dot(turned * masks[t], right)
            for half in range(2):
                slopes[half][pl.ds(chunk * G * PITCH + t, G, stride=PITCH), :] = value[:, half * G : (half + 1) * G]

    def backward(step, behind):
        behind = list(behind)
        base = (count - batch - step * batch) * PITCH
        gaps = [None] * (2 * groups)
        for inner in range(batch - 1, -1, -1):
            for group in range(groups):
                rows = pl.ds(base + (group * count + inner) * PITCH, 8)
                ahead = pl.ds(base + (group * count + max(inner - 1, 0)) * PITCH, 8)
                for half in range(2):
                    at = group * 2 + half
                    gap = slopes[half][rows, :] - behind[at] if gaps[at] is None else gaps[at]
                    moved[half][rows, :] = weights[half][rows, :] * gap
                    step_up = alphas[half][rows, :] * gap
                    gaps[at] = (slopes[half][ahead, :] - behind[at]) - step_up
                    behind[at] = behind[at] + step_up
        return tuple(behind)

    zeros = jnp.zeros((8, G), F32)
    lax.fori_loop(0, count // batch, backward, (zeros,) * (2 * groups))

    pair = 2
    for group in range(groups):
        for t in range(8):
            own = g_own[(group * 8 + t) * 16 : (group * 8 + t + 1) * 16, :]
            for k0 in range(0, kmax, pair):
                span = pair * G
                values = []
                for k in range(k0, k0 + pair):
                    rows = pl.ds((group * kmax + k) * G * PITCH + t, G, stride=PITCH)
                    values.append(jnp.concatenate([moved[0][rows, :].T, moved[1][rows, :].T], axis=0))
                v_high, v_low = split2(jnp.concatenate(values, axis=1))
                table = mono_t[...]
                sums = dot(table, v_high) + dot(table, v_low)
                kept = ((group * 8 + t) * kmax + k0) * G
                tints = dot_t(own, wt_h[kept : kept + span, :]) + dot_t(own, wt_l[kept : kept + span, :])
                for k in range(k0, k0 + pair):
                    spot = place(group, k, t)
                    side = slice((k - k0) * G, (k - k0 + 1) * G)
                    mom[spot * PITCH : spot * PITCH + 8, :] = sums[0:8, side]
                    mat_c[spot * 16 : (spot + 1) * 16, :] = tints[:, side]

    sum_0, sum_x, sum_y, sum_xx, sum_xy, sum_yy = [mom[pl.ds(i, picks, stride=PITCH), :] for i in range(6)]
    off_x, off_y, con_a, con_b, con_c, opac = [feature(i) for i in range(6)]
    cen_x = sum_x - off_x * sum_0
    cen_y = sum_y - off_y * sum_0
    cen_xx = sum_xx - off_x * (sum_x + cen_x)
    cen_yy = sum_yy - off_y * (sum_y + cen_y)
    cen_xy = sum_xy - off_x * sum_y - off_y * cen_x
    outs = [
        con_a * cen_x + con_b * cen_y,
        con_b * cen_x + con_c * cen_y,
        -0.5 * cen_xx,
        -cen_xy,
        -0.5 * cen_yy,
        sum_0 / opac,
    ]
    for channel in range(3):
        outs.append(
            mat_c[pl.ds(channel, picks, stride=16), :] + mat_c[pl.ds(3 + channel, picks, stride=16), :]
        )
    for index, value in enumerate(outs):
        raw[pl.ds(index, picks, stride=16), :] = value

    grad_ref[...] = jnp.zeros(grad_ref.shape, F32)
    for group in range(groups):
        for k in range(kmax):
            for t in range(8):
                slot = jnp.maximum(slots[k, group * 8 + t], 0)
                where = pl.ds((slot // cap) * stride + (slot % cap) * FEAT, FEAT)
                spot = place(group, k, t) * 16
                grad_ref[where, :] = grad_ref[where, :] + raw[spot : spot + FEAT, :]
    grad_ref[pl.ds(stride - 1, scene, stride=stride), :] = jnp.broadcast_to(expo_row, (scene, G))


def vmem():
    return pl.BlockSpec(memory_space=pltpu.VMEM)


def smem():
    return pl.BlockSpec(memory_space=pltpu.SMEM)


def across(rows, axis, parts):
    shaped = rows.reshape(parts, rows.shape[0] // parts, 1, G)
    moved = lax.all_to_all(shaped, axis, split_axis=0, concat_axis=0, tiled=True)
    return moved.reshape(rows.shape)


def near(rows):
    return pltpu.with_memory_space_constraint(rows, pltpu.VMEM)


def render(tile_ids, slots, expo, incoming, goal, interpret=False):
    kmax, tiles = slots.shape
    picks = tiles * kmax
    groups = tiles // 8
    scene = incoming.shape[0] // (2 * FEAT)
    big = pltpu.VMEM((picks // 8 * G * PITCH, G), F32)
    return pl.pallas_call(
        render_kernel,
        out_shape=(
            jax.ShapeDtypeStruct((3, tiles, PIX), F32),
            pltpu.VMEM((scene * (2 * FEAT + 1), G), F32),
        ),
        in_specs=[smem(), smem(), smem(), vmem(), vmem()],
        out_specs=(vmem(), vmem()),
        scratch_shapes=[
            pltpu.VMEM((picks * 16, G), F32),
            pltpu.VMEM((picks * ROWS, G), F32),
            pltpu.VMEM((picks * 16, G), F32),
            pltpu.VMEM((picks * 16, G), BF16),
            pltpu.VMEM((groups * kmax * G, 8 * ROWS), BF16),
            pltpu.VMEM((8 * ROWS, PIX), BF16),
            pltpu.VMEM((16, PIX), BF16),
            big,
            big,
            big,
            big,
            big,
            big,
            big,
            big,
            pltpu.VMEM((picks * G, PIX), BF16),
            pltpu.VMEM((picks * G, PIX), BF16),
            pltpu.VMEM((3 * tiles, PIX), F32),
            pltpu.VMEM((tiles * 16, G), F32),
            pltpu.VMEM((tiles * ROWS, PIX), BF16),
            pltpu.VMEM((tiles * 16, PIX), BF16),
            pltpu.VMEM((picks * PITCH, G), F32),
        ],
        compiler_params=pltpu.CompilerParams(vmem_limit_bytes=56 * 1024 * 1024),
        name="render",
        interpret=interpret,
    )(tile_ids, slots, expo, incoming, goal)


def local(
    means,
    log_scales,
    rotations,
    opacity_logits,
    colour_coefs,
    cameras,
    exposure,
    target,
    tile_ids,
    send_list,
    pair_slots,
):
    views = lax.axis_size("view")
    scene = lax.axis_size("scene")
    blocks = means.shape[0]
    cap = send_list.shape[3]
    pieces = (
        means.transpose(1, 0, 2),
        log_scales.transpose(1, 0, 2),
        rotations,
        opacity_logits,
        colour_coefs,
    )
    picks = send_list[0, 0].T
    own_count = views * blocks * FEAT
    own_proj, kept, cams, picks = pl.pallas_call(
        project_kernel,
        out_shape=(
            pltpu.VMEM((own_count, G), F32),
            pltpu.VMEM((blocks * KEPT, G), F32),
            pltpu.VMEM(cameras.shape, F32),
            pltpu.VMEM(picks.shape, picks.dtype),
        ),
        in_specs=[vmem()] * 7,
        out_specs=(vmem(),) * 4,
        name="project",
    )(*pieces, cameras, picks)
    projected = across(own_proj, "view", views)
    outgoing = pl.pallas_call(
        gather_kernel,
        out_shape=pltpu.VMEM((scene * cap * FEAT, G), F32),
        in_specs=[vmem(), vmem()],
        out_specs=vmem(),
        name="gather",
    )(near(picks), near(projected))
    incoming = across(outgoing, "scene", scene)
    shown, grad_rows = render(
        tile_ids[0], pair_slots[0].T, exposure, near(incoming), near(target[0].transpose(1, 0, 2))
    )
    returned = across(grad_rows, "scene", scene)
    grad_proj, grad_expo = pl.pallas_call(
        scatter_kernel,
        out_shape=(pltpu.VMEM((own_count, G), F32), jax.ShapeDtypeStruct((1, 12), F32)),
        in_specs=[vmem(), vmem()],
        out_specs=(vmem(), vmem()),
        name="scatter",
    )(near(picks), near(returned))
    sent_back = across(grad_proj, "view", views)
    grads = pl.pallas_call(
        unproject_kernel,
        out_shape=tuple(jax.ShapeDtypeStruct(piece.shape, F32) for piece in pieces),
        in_specs=[vmem()] * 3,
        out_specs=tuple(vmem() for _ in pieces),
        name="unproject",
    )(near(kept), near(cams), near(sent_back))
    g_means, g_scales, g_rot, g_logits, g_coefs = grads
    return (
        shown.transpose(1, 0, 2)[None],
        g_means.transpose(1, 0, 2),
        g_scales.transpose(1, 0, 2),
        g_rot,
        g_logits,
        g_coefs,
        grad_expo,
    )


def solution(mesh):
    return jax.shard_map(
        local,
        mesh=mesh,
        in_specs=(
            P(("view", "scene"), None, None),
            P(("view", "scene"), None, None),
            P(("view", "scene"), None, None),
            P(("view", "scene"), None, None),
            P(("view", "scene"), None, None),
            P(),
            P("view", None),
            P("view", "scene", None, None),
            P("view", "scene"),
            P("view", "scene", None, None),
            P("view", "scene", None),
        ),
        out_specs=(
            P("view", "scene", None, None),
            P(("view", "scene"), None, None),
            P(("view", "scene"), None, None),
            P(("view", "scene"), None, None),
            P(("view", "scene"), None, None),
            P(("view", "scene"), None, None),
            P("view", None),
        ),
        check_vma=False,
    )
```

```python
import jax
import jax.numpy as jnp
from jax import lax
from jax.experimental import pallas as pl
from jax.experimental.pallas import tpu as pltpu
from jax.sharding import PartitionSpec as P

PIX = 256
TILE_COLS = 32
G = 128
FEAT = 9
F32 = jnp.float32
BF16 = jnp.bfloat16
LOG2E = 1.4426950408889634

SH_ZERO = 0.28209479177387814
SH_ONE = 0.4886025119029199
SH_TWO = (
    1.0925484305920792,
    -1.0925484305920792,
    0.31539156525252005,
    -1.0925484305920792,
    0.5462742152960396,
)
SH_THREE = (
    -0.5900435899266435,
    2.890611442640554,
    -0.4570457994644658,
    0.3731763325901154,
    -0.4570457994644658,
    1.445305721320277,
    -0.5900435899266435,
)


def harmonics(dir_x, dir_y, dir_z):
    sq_x, sq_y, sq_z = (dir_x * dir_x, dir_y * dir_y, dir_z * dir_z)
    return [
        SH_ZERO * jnp.ones_like(dir_x),
        -SH_ONE * dir_y,
        SH_ONE * dir_z,
        -SH_ONE * dir_x,
        SH_TWO[0] * dir_x * dir_y,
        SH_TWO[1] * dir_y * dir_z,
        SH_TWO[2] * (2.0 * sq_z - sq_x - sq_y),
        SH_TWO[3] * dir_x * dir_z,
        SH_TWO[4] * (sq_x - sq_y),
        SH_THREE[0] * dir_y * (3.0 * sq_x - sq_y),
        SH_THREE[1] * dir_x * dir_y * dir_z,
        SH_THREE[2] * dir_y * (4.0 * sq_z - sq_x - sq_y),
        SH_THREE[3] * dir_z * (2.0 * sq_z - 3.0 * sq_x - 3.0 * sq_y),
        SH_THREE[4] * dir_x * (4.0 * sq_z - sq_x - sq_y),
        SH_THREE[5] * dir_z * (sq_x - sq_y),
        SH_THREE[6] * dir_x * (sq_x - 3.0 * sq_y),
    ]


def project(position, log_scales, quats, logit, coefs, cam):
    rotation = [[cam[3 * row + col] for col in range(3)] for row in range(3)]
    translation = cam[9:12]
    focal_x, focal_y, centre_x, centre_y = cam[12:16]
    view_pos = [
        rotation[row][0] * position[0]
        + rotation[row][1] * position[1]
        + rotation[row][2] * position[2]
        + translation[row]
        for row in range(3)
    ]
    inv_depth = 1.0 / view_pos[2]
    quat_w = quats[0] + 3.0
    quat_x, quat_y, quat_z = quats[1:4]
    quat_norm = jnp.sqrt(quat_w * quat_w + quat_x * quat_x + quat_y * quat_y + quat_z * quat_z)
    inv_norm = 1.0 / quat_norm
    quat_w, quat_x, quat_y, quat_z = (
        quat_w * inv_norm,
        quat_x * inv_norm,
        quat_y * inv_norm,
        quat_z * inv_norm,
    )
    spin = [
        [
            1.0 - 2.0 * (quat_y * quat_y + quat_z * quat_z),
            2.0 * (quat_x * quat_y - quat_w * quat_z),
            2.0 * (quat_x * quat_z + quat_w * quat_y),
        ],
        [
            2.0 * (quat_x * quat_y + quat_w * quat_z),
            1.0 - 2.0 * (quat_x * quat_x + quat_z * quat_z),
            2.0 * (quat_y * quat_z - quat_w * quat_x),
        ],
        [
            2.0 * (quat_x * quat_z - quat_w * quat_y),
            2.0 * (quat_y * quat_z + quat_w * quat_x),
            1.0 - 2.0 * (quat_x * quat_x + quat_y * quat_y),
        ],
    ]
    scales = [jnp.exp(row) for row in log_scales]
    world = [[spin[row][col] * scales[col] for col in range(3)] for row in range(3)]
    step_x = focal_x * inv_depth
    step_y = focal_y * inv_depth
    slide_x = step_x * view_pos[0] * inv_depth
    slide_y = step_y * view_pos[1] * inv_depth
    jac = [
        [step_x * rotation[0][col] - slide_x * rotation[2][col] for col in range(3)],
        [step_y * rotation[1][col] - slide_y * rotation[2][col] for col in range(3)],
    ]
    screen = [
        [
            jac[row][0] * world[0][col] + jac[row][1] * world[1][col] + jac[row][2] * world[2][col]
            for col in range(3)
        ]
        for row in range(2)
    ]
    sigma_xx = screen[0][0] * screen[0][0] + screen[0][1] * screen[0][1] + screen[0][2] * screen[0][2] + 0.3
    sigma_yy = screen[1][0] * screen[1][0] + screen[1][1] * screen[1][1] + screen[1][2] * screen[1][2] + 0.3
    sigma_xy = screen[0][0] * screen[1][0] + screen[0][1] * screen[1][1] + screen[0][2] * screen[1][2]
    inv_det = 1.0 / (sigma_xx * sigma_yy - sigma_xy * sigma_xy)
    screen_x = step_x * view_pos[0] + centre_x
    screen_y = step_y * view_pos[1] + centre_y
    opacity = 1.0 / (1.0 + jnp.exp(-logit))
    eye = [
        -(
            rotation[0][col] * translation[0]
            + rotation[1][col] * translation[1]
            + rotation[2][col] * translation[2]
        )
        for col in range(3)
    ]
    offs = [position[col] - eye[col] for col in range(3)]
    inv_dist = 1.0 / jnp.sqrt(offs[0] * offs[0] + offs[1] * offs[1] + offs[2] * offs[2])
    basis = harmonics(offs[0] * inv_dist, offs[1] * inv_dist, offs[2] * inv_dist)
    colours = []
    for channel in range(3):
        total = basis[0] * coefs[channel]
        for band in range(1, 16):
            total = total + basis[band] * coefs[3 * band + channel]
        colours.append(jnp.maximum(0.5 + total, 0.0))
    return [
        screen_x,
        screen_y,
        sigma_yy * inv_det,
        -sigma_xy * inv_det,
        sigma_xx * inv_det,
        opacity,
    ] + colours


KEPT = 64


def block_inputs(kept, block, views):
    def rows(first, count):
        start = block * KEPT + first
        return [jnp.broadcast_to(kept[start + r : start + r + 1, :], (views, G)) for r in range(count)]

    return (rows(0, 3), rows(3, 3), rows(6, 4), rows(10, 1)[0], rows(16, 48))


def camera_columns(cam_ref, views):
    cams = cam_ref[...]
    return [jnp.broadcast_to(cams[:, col : col + 1], (views, G)) for col in range(16)]


def project_kernel(
    means, log_scales, rotations, logits, coefs, cam_ref, picks, out_ref, kept, cam_kept, picks_kept
):
    views = cam_ref.shape[0]
    blocks = rotations.shape[0]
    cam_kept[...] = cam_ref[...]
    picks_kept[...] = picks[...]
    cam = camera_columns(cam_ref, views)
    for block in range(blocks):
        start = block * KEPT
        for r in range(3):
            kept[start + r : start + r + 1, :] = means[r, pl.ds(block, 1), :]
            kept[start + 3 + r : start + 4 + r, :] = log_scales[r, pl.ds(block, 1), :]
        kept[start + 6 : start + 10, :] = rotations[block]
        kept[start + 10 : start + 11, :] = logits[block]
        kept[start + 11 : start + 16, :] = jnp.zeros((5, G), F32)
        kept[start + 16 : start + KEPT, :] = coefs[block]
        for feat, value in enumerate(project(*block_inputs(kept, block, views), cam)):
            out_ref[pl.ds(block * FEAT + feat, views, stride=blocks * FEAT), :] = value


def unproject_kernel(kept, cam_ref, back_ref, o_means, o_scales, o_rot, o_logit, o_coef):
    views = cam_ref.shape[0]
    blocks = o_rot.shape[0]
    cam = camera_columns(cam_ref, views)

    def total(value):
        return jnp.sum(value, axis=0, keepdims=True)

    for block in range(blocks):
        pieces = block_inputs(kept, block, views)
        _, pull = jax.vjp(lambda *own: project(*own, cam), *pieces)
        seeds = [
            back_ref[pl.ds(block * FEAT + feat, views, stride=blocks * FEAT), :] for feat in range(FEAT)
        ]
        g_means, g_scales, g_rot, g_logit, g_coef = pull(seeds)
        for ref, rows in ((o_means, g_means), (o_scales, g_scales)):
            for row, value in enumerate(rows):
                ref[row, pl.ds(block, 1), :] = total(value)
        for ref, rows in ((o_rot, g_rot), (o_logit, [g_logit]), (o_coef, g_coef)):
            for row, value in enumerate(rows):
                ref[block, pl.ds(row, 1), :] = total(value)


def chosen(picks, cap, blocks):
    spots = lax.broadcasted_iota(jnp.int32, (blocks, picks.shape[1]), 0)
    return [jnp.where(spots == picks[c : c + 1, :], 1.0, 0.0) for c in range(cap)]


def gather_kernel(picks, src_ref, out_ref):
    cap, renderers = picks.shape
    blocks = src_ref.shape[0] // FEAT
    turned = [select.T.astype(BF16) for select in chosen(jnp.maximum(picks[...], 0), cap, blocks)]
    for feat in range(FEAT):
        pieces = [piece.astype(BF16) for piece in pieces3(src_ref[pl.ds(feat, blocks, stride=FEAT), :])]
        for c in range(cap):
            value = dot(turned[c], pieces[0]) + dot(turned[c], pieces[1]) + dot(turned[c], pieces[2])
            out_ref[pl.ds(c * FEAT + feat, renderers, stride=cap * FEAT), :] = value


def scatter_kernel(picks, src_ref, out_ref, expo_ref):
    cap, renderers = picks.shape
    stride = cap * FEAT + 1
    blocks = out_ref.shape[0] // FEAT
    selects = [select.astype(BF16) for select in chosen(picks[...], cap, blocks)]
    for feat in range(FEAT):
        total = jnp.zeros((blocks, G), F32)
        for c in range(cap):
            rows = src_ref[pl.ds(c * FEAT + feat, renderers, stride=stride), :]
            for piece in pieces3(rows):
                total = total + dot(selects[c], piece.astype(BF16))
        out_ref[pl.ds(feat, blocks, stride=FEAT), :] = total
    terms = src_ref[pl.ds(stride - 1, renderers, stride=stride), :]
    expo_ref[...] = jnp.sum(terms, axis=0, keepdims=True)[:, 0:12]


def split2(value):
    high = value.astype(BF16)
    low = (value - high.astype(F32)).astype(BF16)
    return high, low


def pieces3(value):
    high = value.astype(BF16).astype(F32)
    rest = value - high
    middle = rest.astype(BF16).astype(F32)
    return high, middle, rest - middle


def monomials(part, pixel):
    spot_x = (pixel % 16).astype(F32) - 7.5
    spot_y = (pixel // 16).astype(F32) - 7.5
    value = jnp.where(part == 0, 1.0, 0.0)
    value = jnp.where(part == 1, spot_x, value)
    value = jnp.where(part == 2, spot_y, value)
    value = jnp.where(part == 3, spot_x * spot_x, value)
    value = jnp.where(part == 4, spot_x * spot_y, value)
    return jnp.where(part == 5, spot_y * spot_y, value)


def dot(left, right):
    return jnp.dot(left, right, preferred_element_type=F32)


def dot_t(left, right):
    return lax.dot_general(left, right, (((1,), (1,)), ((), ())), preferred_element_type=F32)


ROWS = 32
PITCH = 9


def render_kernel(
    tile_ids,
    slots,
    expo,
    in_ref,
    goal_ref,
    shown_ref,
    grad_ref,
    raw,
    mat,
    mat_c,
    mat_b,
    left,
    mono,
    mono_t,
    al0,
    al1,
    wt0,
    wt1,
    gm0,
    gm1,
    hh0,
    hh1,
    wt_h,
    wt_l,
    ccol,
    gall,
    g_rhs,
    g_own,
    mom,
):
    kmax, tiles = slots.shape
    groups = tiles // 8
    picks = tiles * kmax
    cap = 2
    stride = cap * FEAT + 1
    scene = grad_ref.shape[0] // stride
    wide = 8 * ROWS
    rows16 = lax.broadcasted_iota(jnp.int32, (16, G), 0)
    lanes = lax.broadcasted_iota(jnp.int32, (1, G), 1)
    alphas, weights, slopes, moved = (al0, al1), (wt0, wt1), (gm0, gm1), (hh0, hh1)

    row = lax.broadcasted_iota(jnp.int32, (wide, PIX), 0) // 8
    part = jnp.where(row < 18, row % 6, 6)
    mono[...] = monomials(part, lax.broadcasted_iota(jnp.int32, (wide, PIX), 1)).astype(BF16)
    part = lax.broadcasted_iota(jnp.int32, (16, PIX), 0)
    mono_t[...] = monomials(part, lax.broadcasted_iota(jnp.int32, (16, PIX), 1)).astype(BF16)

    def place(group, k, t):
        return (group * kmax + k) * 8 + t

    for group in range(groups):
        for t in range(8):
            tile = group * 8 + t
            tile_id = tile_ids[tile]
            mid_x = ((tile_id % TILE_COLS) * 16 + 8).astype(F32)
            mid_y = ((tile_id // TILE_COLS) * 16 + 8).astype(F32)
            shift = jnp.where(rows16 == 0, mid_x, jnp.where(rows16 == 1, mid_y, 0.0))
            for k in range(kmax):
                slot = slots[k, tile]
                base = jnp.maximum(slot, 0) * FEAT
                spot = place(group, k, t) * 16
                raw[spot : spot + FEAT, :] = in_ref[pl.ds(base, FEAT), :] - shift[0:FEAT]
                raw[spot + FEAT : spot + FEAT + 1, :] = jnp.full((1, G), jnp.where(slot < 0, -4000.0, 0.0))

    def feature(index):
        return raw[pl.ds(index, picks, stride=16), :]

    off_x, off_y, con_a, con_b, con_c, opac = [feature(i) for i in range(6)]
    poly_a = con_a * (-0.5 * LOG2E)
    poly_b = con_b * (-LOG2E)
    poly_c = con_c * (-0.5 * LOG2E)
    lead = poly_a * off_x + poly_b * off_y
    tail = poly_c * off_y
    coefs = [
        off_x * lead + off_y * tail + jnp.log(opac) * LOG2E + feature(FEAT),
        -(lead + poly_a * off_x),
        -(2.0 * tail + poly_b * off_x),
        poly_a,
        poly_b,
        poly_c,
    ]
    blank = jnp.zeros((8, G), F32)
    rows_of = [blank] * ROWS
    for index in range(6):
        for piece, value in enumerate(pieces3(coefs[index])):
            rows_of[6 * piece + index] = value
    mat_c[...] = jnp.zeros(mat_c.shape, F32)
    for channel in range(3):
        high, middle, _ = pieces3(feature(6 + channel))
        rows_of[18 + channel] = high
        rows_of[21 + channel] = middle
        rows_of[24 + channel] = high
        mat_c[pl.ds(channel, picks, stride=16), :] = high
        mat_c[pl.ds(3 + channel, picks, stride=16), :] = middle
    for chunk in range(groups * kmax):
        for index, value in enumerate(rows_of):
            start = chunk * wide + index * 8
            mat[start : start + 8, :] = value if index >= 27 else value[chunk * 8 : chunk * 8 + 8]
    mat_b[...] = mat_c[...].astype(BF16)

    lane_tile = lax.broadcasted_iota(jnp.int32, (1, wide), 1) % 8
    masks = [jnp.where(lane_tile == t, 1.0, 0.0).astype(BF16) for t in range(8)]

    for chunk in range(groups * kmax):
        sides = [mat[chunk * wide + half * G : chunk * wide + (half + 1) * G, :].T for half in range(2)]
        turned = jnp.concatenate(sides, axis=1).astype(BF16)
        left[chunk * G : (chunk + 1) * G, :] = turned
        for t in range(8):
            alpha = jnp.exp2(dot(turned * masks[t], mono[...]))
            for half in range(2):
                alphas[half][pl.ds(chunk * G * PITCH + t, G, stride=PITCH), :] = alpha[:, half * G : (half + 1) * G]

    count = kmax * G

    batch = 32

    def forward(step, keeps):
        keeps = list(keeps)
        base = step * (batch * PITCH)
        for inner in range(batch):
            for group in range(groups):
                rows = pl.ds(base + (group * count + inner) * PITCH, 8)
                for half in range(2):
                    at = group * 2 + half
                    alpha = alphas[half][rows, :]
                    weights[half][rows, :] = keeps[at] * alpha
                    keeps[at] = keeps[at] * (1.0 - alpha)
        return tuple(keeps)

    ones = jnp.ones((8, G), F32)
    lax.fori_loop(0, count // batch, forward, (ones,) * (2 * groups))

    for group in range(groups):
        for t in range(8):
            total = jnp.zeros((16, PIX), F32)
            for k in range(kmax):
                spot = place(group, k, t)
                rows = pl.ds((group * kmax + k) * G * PITCH + t, G, stride=PITCH)
                weight = jnp.concatenate([weights[0][rows, :], weights[1][rows, :]], axis=1)
                w_high, w_low = split2(weight)
                kept = ((group * 8 + t) * kmax + k) * G
                wt_h[kept : kept + G, :] = w_high
                wt_l[kept : kept + G, :] = w_low
                own = mat_b[spot * 16 : (spot + 1) * 16, :]
                total = total + dot(own, wt_h[kept : kept + G, :])
                total = total + dot(own, wt_l[kept : kept + G, :])
            for channel in range(3):
                row = channel * tiles + group * 8 + t
                ccol[row : row + 1, :] = total[channel : channel + 1, :] + total[3 + channel : 4 + channel, :]

    colour = [ccol[c * tiles : (c + 1) * tiles, :] for c in range(3)]
    miss = []
    for i in range(3):
        value = colour[i] + expo[0, 9 + i]
        for j in range(3):
            value = value + expo[0, 3 * i + j] * colour[j]
        shown_ref[i] = value
        miss.append(value - goal_ref[i])
    slope = []
    for j in range(3):
        value = miss[j]
        for i in range(3):
            value = value + expo[0, 3 * i + j] * miss[i]
        slope.append(value)
    terms = [miss[i] * colour[j] for i in range(3) for j in range(3)] + miss
    expo_row = jnp.zeros((1, G), F32)
    for index, value in enumerate(terms):
        folded = jnp.sum(value[:, 0:G] + value[:, G : 2 * G], axis=0, keepdims=True)
        expo_row = jnp.where(lanes == index, jnp.sum(folded, axis=1, keepdims=True), expo_row)

    highs = [value.astype(BF16).astype(F32) for value in slope]
    lows = [value - high for value, high in zip(slope, highs)]
    for group in range(groups):
        span = slice(group * 8, group * 8 + 8)
        nine = [value[span] for value in highs + highs + lows]
        stack = [jnp.zeros((18 * 8, PIX), F32)] + nine + [jnp.zeros(((ROWS - 27) * 8, PIX), F32)]
        g_rhs[group * wide : (group + 1) * wide, :] = jnp.concatenate(stack, axis=0).astype(BF16)
    gall[...] = jnp.zeros(gall.shape, F32)
    for half in range(2):
        side = slice(half * G, (half + 1) * G)
        for channel in range(3):
            gall[pl.ds(channel, tiles, stride=16), :] = highs[channel][:, side]
            gall[pl.ds(3 + channel, tiles, stride=16), :] = lows[channel][:, side]
        g_own[:, side] = gall[...].astype(BF16)
    for chunk in range(groups * kmax):
        turned = left[chunk * G : (chunk + 1) * G, :]
        group = chunk // kmax
        right = g_rhs[group * wide : (group + 1) * wide, :]
        for t in range(8):
            value = dot(turned * masks[t], right)
            for half in range(2):
                slopes[half][pl.ds(chunk * G * PITCH + t, G, stride=PITCH), :] = value[:, half * G : (half + 1) * G]

    def backward(step, behind):
        behind = list(behind)
        base = (count - batch - step * batch) * PITCH
        gaps = [None] * (2 * groups)
        for inner in range(batch - 1, -1, -1):
            for group in range(groups):
                rows = pl.ds(base + (group * count + inner) * PITCH, 8)
                ahead = pl.ds(base + (group * count + max(inner - 1, 0)) * PITCH, 8)
                for half in range(2):
                    at = group * 2 + half
                    gap = slopes[half][rows, :] - behind[at] if gaps[at] is None else gaps[at]
                    moved[half][rows, :] = weights[half][rows, :] * gap
                    step_up = alphas[half][rows, :] * gap
                    gaps[at] = (slopes[half][ahead, :] - behind[at]) - step_up
                    behind[at] = behind[at] + step_up
        return tuple(behind)

    zeros = jnp.zeros((8, G), F32)
    lax.fori_loop(0, count // batch, backward, (zeros,) * (2 * groups))

    pair = 2
    for group in range(groups):
        for t in range(8):
            own = g_own[(group * 8 + t) * 16 : (group * 8 + t + 1) * 16, :]
            for k0 in range(0, kmax, pair):
                span = pair * G
                values = []
                for k in range(k0, k0 + pair):
                    rows = pl.ds((group * kmax + k) * G * PITCH + t, G, stride=PITCH)
                    values.append(jnp.concatenate([moved[0][rows, :].T, moved[1][rows, :].T], axis=0))
                v_high, v_low = split2(jnp.concatenate(values, axis=1))
                table = mono_t[...]
                sums = dot(table, v_high) + dot(table, v_low)
                kept = ((group * 8 + t) * kmax + k0) * G
                tints = dot_t(own, wt_h[kept : kept + span, :]) + dot_t(own, wt_l[kept : kept + span, :])
                for k in range(k0, k0 + pair):
                    spot = place(group, k, t)
                    side = slice((k - k0) * G, (k - k0 + 1) * G)
                    mom[spot * PITCH : spot * PITCH + 8, :] = sums[0:8, side]
                    mat_c[spot * 16 : (spot + 1) * 16, :] = tints[:, side]

    sum_0, sum_x, sum_y, sum_xx, sum_xy, sum_yy = [mom[pl.ds(i, picks, stride=PITCH), :] for i in range(6)]
    off_x, off_y, con_a, con_b, con_c, opac = [feature(i) for i in range(6)]
    cen_x = sum_x - off_x * sum_0
    cen_y = sum_y - off_y * sum_0
    cen_xx = sum_xx - off_x * (sum_x + cen_x)
    cen_yy = sum_yy - off_y * (sum_y + cen_y)
    cen_xy = sum_xy - off_x * sum_y - off_y * cen_x
    outs = [
        con_a * cen_x + con_b * cen_y,
        con_b * cen_x + con_c * cen_y,
        -0.5 * cen_xx,
        -cen_xy,
        -0.5 * cen_yy,
        sum_0 / opac,
    ]
    for channel in range(3):
        outs.append(
            mat_c[pl.ds(channel, picks, stride=16), :] + mat_c[pl.ds(3 + channel, picks, stride=16), :]
        )
    for index, value in enumerate(outs):
        raw[pl.ds(index, picks, stride=16), :] = value

    grad_ref[...] = jnp.zeros(grad_ref.shape, F32)
    for group in range(groups):
        for k in range(kmax):
            for t in range(8):
                slot = jnp.maximum(slots[k, group * 8 + t], 0)
                where = pl.ds((slot // cap) * stride + (slot % cap) * FEAT, FEAT)
                spot = place(group, k, t) * 16
                grad_ref[where, :] = grad_ref[where, :] + raw[spot : spot + FEAT, :]
    grad_ref[pl.ds(stride - 1, scene, stride=stride), :] = jnp.broadcast_to(expo_row, (scene, G))


def vmem():
    return pl.BlockSpec(memory_space=pltpu.VMEM)


def smem():
    return pl.BlockSpec(memory_space=pltpu.SMEM)


def across(rows, axis, parts):
    shaped = rows.reshape(parts, rows.shape[0] // parts, 1, G)
    moved = lax.all_to_all(shaped, axis, split_axis=0, concat_axis=0, tiled=True)
    return moved.reshape(rows.shape)


def near(rows):
    return pltpu.with_memory_space_constraint(rows, pltpu.VMEM)


def render(tile_ids, slots, expo, incoming, goal, interpret=False):
    kmax, tiles = slots.shape
    picks = tiles * kmax
    groups = tiles // 8
    scene = incoming.shape[0] // (2 * FEAT)
    big = pltpu.VMEM((picks // 8 * G * PITCH, G), F32)
    return pl.pallas_call(
        render_kernel,
        out_shape=(
            jax.ShapeDtypeStruct((3, tiles, PIX), F32),
            pltpu.VMEM((scene * (2 * FEAT + 1), G), F32),
        ),
        in_specs=[smem(), smem(), smem(), vmem(), vmem()],
        out_specs=(vmem(), vmem()),
        scratch_shapes=[
            pltpu.VMEM((picks * 16, G), F32),
            pltpu.VMEM((picks * ROWS, G), F32),
            pltpu.VMEM((picks * 16, G), F32),
            pltpu.VMEM((picks * 16, G), BF16),
            pltpu.VMEM((groups * kmax * G, 8 * ROWS), BF16),
            pltpu.VMEM((8 * ROWS, PIX), BF16),
            pltpu.VMEM((16, PIX), BF16),
            big,
            big,
            big,
            big,
            big,
            big,
            big,
            big,
            pltpu.VMEM((picks * G, PIX), BF16),
            pltpu.VMEM((picks * G, PIX), BF16),
            pltpu.VMEM((3 * tiles, PIX), F32),
            pltpu.VMEM((tiles * 16, G), F32),
            pltpu.VMEM((tiles * ROWS, PIX), BF16),
            pltpu.VMEM((tiles * 16, PIX), BF16),
            pltpu.VMEM((picks * PITCH, G), F32),
        ],
        compiler_params=pltpu.CompilerParams(vmem_limit_bytes=56 * 1024 * 1024),
        name="render",
        interpret=interpret,
    )(tile_ids, slots, expo, incoming, goal)


def local(
    means,
    log_scales,
    rotations,
    opacity_logits,
    colour_coefs,
    cameras,
    exposure,
    target,
    tile_ids,
    send_list,
    pair_slots,
):
    views = lax.axis_size("view")
    scene = lax.axis_size("scene")
    blocks = means.shape[0]
    cap = send_list.shape[3]
    pieces = (
        means.transpose(1, 0, 2),
        log_scales.transpose(1, 0, 2),
        rotations,
        opacity_logits,
        colour_coefs,
    )
    picks = send_list[0, 0].T
    own_count = views * blocks * FEAT
    own_proj, kept, cams, picks = pl.pallas_call(
        project_kernel,
        out_shape=(
            pltpu.VMEM((own_count, G), F32),
            pltpu.VMEM((blocks * KEPT, G), F32),
            pltpu.VMEM(cameras.shape, F32),
            pltpu.VMEM(picks.shape, picks.dtype),
        ),
        in_specs=[vmem()] * 7,
        out_specs=(vmem(),) * 4,
        name="project",
    )(*pieces, cameras, picks)
    projected = across(own_proj, "view", views)
    outgoing = pl.pallas_call(
        gather_kernel,
        out_shape=pltpu.VMEM((scene * cap * FEAT, G), F32),
        in_specs=[vmem(), vmem()],
        out_specs=vmem(),
        name="gather",
    )(near(picks), near(projected))
    incoming = across(outgoing, "scene", scene)
    shown, grad_rows = render(
        tile_ids[0], pair_slots[0].T, exposure, near(incoming), near(target[0].transpose(1, 0, 2))
    )
    returned = across(grad_rows, "scene", scene)
    grad_proj, grad_expo = pl.pallas_call(
        scatter_kernel,
        out_shape=(pltpu.VMEM((own_count, G), F32), jax.ShapeDtypeStruct((1, 12), F32)),
        in_specs=[vmem(), vmem()],
        out_specs=(vmem(), vmem()),
        name="scatter",
    )(near(picks), near(returned))
    sent_back = across(grad_proj, "view", views)
    grads = pl.pallas_call(
        unproject_kernel,
        out_shape=tuple(jax.ShapeDtypeStruct(piece.shape, F32) for piece in pieces),
        in_specs=[vmem()] * 3,
        out_specs=tuple(vmem() for _ in pieces),
        name="unproject",
    )(near(kept), near(cams), near(sent_back))
    g_means, g_scales, g_rot, g_logits, g_coefs = grads
    return (
        shown.transpose(1, 0, 2)[None],
        g_means.transpose(1, 0, 2),
        g_scales.transpose(1, 0, 2),
        g_rot,
        g_logits,
        g_coefs,
        grad_expo,
    )


def solution(mesh):
    return jax.shard_map(
        local,
        mesh=mesh,
        in_specs=(
            P(("view", "scene"), None, None),
            P(("view", "scene"), None, None),
            P(("view", "scene"), None, None),
            P(("view", "scene"), None, None),
            P(("view", "scene"), None, None),
            P(),
            P("view", None),
            P("view", "scene", None, None),
            P("view", "scene"),
            P("view", "scene", None, None),
            P("view", "scene", None),
        ),
        out_specs=(
            P("view", "scene", None, None),
            P(("view", "scene"), None, None),
            P(("view", "scene"), None, None),
            P(("view", "scene"), None, None),
            P(("view", "scene"), None, None),
            P(("view", "scene"), None, None),
            P("view", None),
        ),
        check_vma=False,
    )
```
